256 devices in a mesh: freq: 8 (over y, core), stcol: 32 (over x, z).
Axes of the slice: x: 4, y: 4, z: 8, core: 2. Of those that a mesh axis runs over, the one named last changes fastest.
Arguments:
- visibilities: float32 [2, 8, 512, 1, 512], P(None, 'freq', 'stcol'), may hold values from -28.8 to 28.8
- positions: float32 [3, 1, 512], replicated, may hold values from -3 to 3
- source_lmn: float32 [3, 1024], replicated, may hold values from -0.5 to 0.5
- source_flux: float32 [1024], replicated, may hold values from 0.02 to 0.2
- cluster_map: int32 [1024], replicated, may hold values from 0 to 15, as said below
- station_order: int32 [512], replicated, may hold values from 0 to 511, each once
- penalty: float32 [16], replicated, may hold values from 9.8304 to 196.608
- offsets: float32 [2, 8, 16, 512], P(None, 'freq'), may hold values from -1.2 to 1.2
Outputs:
- gains: float32 [2, 8, 16, 512], P(None, 'freq', None, 'stcol')
- consensus: float32 [2, 8, 16, 512], P(None, 'freq', None, 'stcol')
The draws below stay inside these ranges and needn't reach their ends.
Inputs may be any that keep to these rules, and one draw needn't show every extreme that they name: `cluster_map`: each of the 16 directions is named by exactly 64 sources. `station_order`: every station stands exactly once.
All inputs are finite; a program needn't handle non-finite values.
Results may differ from the reference program's by a relative error of at most 0.00011.
Values sent between devices are 32-bit elements; how exact they have to be, the bound alone decides.
No kernel may reach another device: no remote copies, remote signals or barrier semaphores. Data moves between devices by JAX's collectives and lax.ppermute only.
A program may use at most 64 MiB of HBM per device.

```python
import math
import jax
import jax.numpy as jnp
from jax import lax

STATIONS = 512
DIRS = 16
SRC_DIR = 64
TIMES = 1
ADMM = 2
PASSES = 2
CHANNELS = 8
SOURCES = 1024


def draw_cluster_map(key, part):
    labels = jnp.arange(DIRS * SRC_DIR, dtype=jnp.int32) // SRC_DIR
    return jax.random.permutation(jax.random.fold_in(key, 11), labels)


def steps_of(stream_key, dims, cuts, low, largest):
    def one(dim, parts):
        heights = jax.random.uniform(jax.random.fold_in(jax.random.fold_in(stream_key, 6), dim), (parts,), jnp.float32, low / len(cuts), largest / len(cuts))
        return jnp.repeat(jnp.exp(heights), dims[dim] // parts).reshape((-1,) + (1,) * (len(dims) - dim - 1))

    loudness = one(*cuts[0])
    for cut in cuts[1:]:
        loudness = loudness * one(*cut)
    return loudness


def bell_draw(rng, extent, spread, reach, cuts=(), held_as=jnp.bfloat16):
    drawn = spread * jax.random.normal(rng, extent, jnp.float32)
    if cuts:
        drawn = drawn * steps_of(rng, extent, cuts, -0.22, 0.18)
    return jnp.clip(drawn, -reach, reach).astype(held_as)


def setup_inputs(seed: int = 0) -> dict:
    arg_keys = jax.random.split(jax.random.key(seed), 9)
    visibilities = bell_draw(arg_keys[0], (2, CHANNELS, STATIONS, TIMES, STATIONS), (0.15 * (DIRS * SRC_DIR) ** 0.5), 28.8, ((1, 8), (2, 32)), jnp.float32)
    positions = bell_draw(arg_keys[1], (3, TIMES, STATIONS), 0.5, 3.0, (), jnp.float32)
    source_lmn = jnp.clip(jax.random.uniform(arg_keys[2], (3, SOURCES), jnp.float32, -0.5, 0.5), -0.5, 0.5)
    source_flux = jnp.clip(jnp.exp(jax.random.uniform(arg_keys[3], (SOURCES,), jnp.float32, math.log(0.02), math.log(0.2))), 0.02, 0.2)
    cluster_map = draw_cluster_map(jax.random.fold_in(arg_keys[8], 71), 0)
    station_order = jax.random.permutation(arg_keys[5], STATIONS).astype(jnp.int32)
    penalty = jnp.clip(jnp.exp(jax.random.uniform(arg_keys[6], (DIRS,), jnp.float32, math.log(9.8304), math.log(196.608))), 9.8304, 196.608)
    offsets = bell_draw(arg_keys[7], (2, CHANNELS, DIRS, STATIONS), 0.2, 1.2, ((1, 8),), jnp.float32)
    return {"visibilities": visibilities, "positions": positions, "source_lmn": source_lmn, "source_flux": source_flux, "cluster_map": cluster_map, "station_order": station_order, "penalty": penalty, "offsets": offsets}


HIGHEST = lax.Precision.HIGHEST

def frequencies(channels):
    return 1.0 + 0.5 * jnp.arange(channels, dtype=jnp.float32) / channels

def basis_table(channels):
    centre = (jnp.arange(channels, dtype=jnp.float32) - 0.5 * (channels - 1)) / channels
    columns = [jnp.ones_like(centre), centre, centre * centre]
    finished = []
    for column in columns:
        for before in finished:
            column = column - jnp.sum(column * before) * before
        finished.append(column / jnp.sqrt(jnp.sum(column * column)))
    return jnp.stack(finished, axis=1)

def group_sources(source_lmn, source_flux, cluster_map, directions):
    ranking = jnp.argsort(cluster_map, stable=True)
    cosines = jnp.take(source_lmn, ranking, axis=1).reshape(3, directions, -1)
    brightness = jnp.take(source_flux, ranking).reshape(directions, -1)
    return (jnp.moveaxis(cosines, 1, 0), brightness)

def contract(row_part, column_part):
    return jnp.einsum('ctps,ctjs->cjtp', row_part, column_part, precision=HIGHEST)

def model_block(positions, direction_cosines, weights, freq_scale, column_ids):
    projected = positions[0][:, :, None] * direction_cosines[0] + positions[1][:, :, None] * direction_cosines[1]
    projected = projected + positions[2][:, :, None] * direction_cosines[2]
    phases = 2.0 * math.pi * freq_scale[:, None, None, None] * projected[None]
    cosine = jnp.cos(phases)
    sine_part = jnp.sin(phases)
    weighted_cos = cosine * weights
    weighted_sin = sine_part * weights
    column_cos = jnp.take(cosine, column_ids, axis=2)
    column_sin = jnp.take(sine_part, column_ids, axis=2)
    model_real = contract(weighted_cos, column_cos) + contract(weighted_sin, column_sin)
    model_imag = contract(weighted_sin, column_cos) - contract(weighted_cos, column_sin)
    station_ids = jnp.arange(positions.shape[2], dtype=jnp.int32)
    retained = (column_ids[:, None] != station_ids[None, :]).astype(model_real.dtype)
    retained = retained[None, :, None, :]
    return (model_real * retained, model_imag * retained)

def gain_update(numerator, denominator, gains, consensus, multiplier, penalty):
    weight_pen = penalty[:, None]
    scaling = 1.0 / (denominator + weight_pen)
    fresh = (numerator + gains * denominator + weight_pen * (consensus - multiplier)) * scaling
    return 0.5 * (gains + fresh)

def polynomial_fit(values, basis):
    coefficients = jnp.einsum('fj,rfkp->rjkp', basis, values, precision=HIGHEST)
    return jnp.einsum('fj,rjkp->rfkp', basis, coefficients, precision=HIGHEST)

def pass_terms(vis_chan, gains, model_real, model_imag, column_ids):
    column_gains = jnp.take(gains, column_ids, axis=3)
    column_real = jnp.moveaxis(column_gains[0], 1, 0)[:, :, :, None, None]
    column_imag = jnp.moveaxis(column_gains[1], 1, 0)[:, :, :, None, None]
    row_real = jnp.moveaxis(gains[0], 1, 0)[:, :, None, None, :]
    row_imag = jnp.moveaxis(gains[1], 1, 0)[:, :, None, None, :]
    along_real = model_real * column_real + model_imag * column_imag
    along_imag = model_imag * column_real - model_real * column_imag
    pred_real = row_real * along_real - row_imag * along_imag
    pred_imag = row_real * along_imag + row_imag * along_real
    resid_real = vis_chan[0] - lax.optimization_barrier(jnp.sum(pred_real, axis=0))
    resid_imag = vis_chan[1] - lax.optimization_barrier(jnp.sum(pred_imag, axis=0))
    num_real = lax.optimization_barrier(jnp.sum(resid_real * along_real + resid_imag * along_imag, axis=(2, 3)))
    num_imag = lax.optimization_barrier(jnp.sum(resid_imag * along_real - resid_real * along_imag, axis=(2, 3)))
    denominator = lax.optimization_barrier(jnp.sum(along_real * along_real + along_imag * along_imag, axis=(2, 3)))
    numerator = jnp.moveaxis(jnp.stack([num_real, num_imag]), 1, 2)
    return (numerator, jnp.moveaxis(denominator, 0, 1)[None])

def reference(visibilities, positions, source_lmn, source_flux, cluster_map, station_order, penalty, offsets):
    channels = visibilities.shape[1]
    directions = penalty.shape[0]
    freq_all = frequencies(channels)
    basis = basis_table(channels)
    cosines, brightness = group_sources(source_lmn, source_flux, cluster_map, directions)
    gains = jnp.stack([1.0 + offsets[0], offsets[1]])
    consensus = gains
    multiplier = jnp.zeros_like(gains)
    for admm_step in range(ADMM):

        def channel_work(items):
            vis_chan, freq_chan, gain_chan, cons_chan, mult_chan = items
            vis_chan = vis_chan[:, None]
            gain_chan = gain_chan[:, None]
            cons_chan = cons_chan[:, None]
            mult_chan = mult_chan[:, None]

            def one_model(entry):
                return model_block(positions, entry[0], entry[1], freq_chan[None], station_order)
            model_real, model_imag = lax.map(one_model, (cosines, brightness))
            for sweep_index in range(PASSES):
                numerator, denominator = pass_terms(vis_chan, gain_chan, model_real, model_imag, station_order)
                gain_chan = gain_update(numerator, denominator, gain_chan, cons_chan, mult_chan, penalty)
            return gain_chan[:, 0]
        solved = lax.map(channel_work, (jnp.moveaxis(visibilities, 1, 0), freq_all, jnp.moveaxis(gains, 1, 0), jnp.moveaxis(consensus, 1, 0), jnp.moveaxis(multiplier, 1, 0)))
        gains = jnp.moveaxis(solved, 0, 1)
        consensus = polynomial_fit(gains + multiplier, basis)
        multiplier = multiplier + gains - consensus
    return (gains, consensus)
```

```python
import math

import jax
import jax.numpy as jnp
import numpy as np
from jax import lax
from jax.experimental import pallas as pl
from jax.experimental.pallas import tpu as pltpu
from jax.sharding import PartitionSpec as P

STATIONS = 512
DIRS = 16
SRC = 64
CHANNELS = 8
GROUP = 32
OWN = 16
LANES = 128
F32 = jnp.float32
BF16 = jnp.bfloat16

COS_TERMS = None
SIN_TERMS = None


def fit_terms():
    nodes = np.cos(np.pi * (np.arange(400) + 0.5) / 400)
    u = 0.125 * (nodes + 1.0)
    r = np.sqrt(u)
    cheb = np.polynomial.chebyshev
    poly = np.polynomial.polynomial

    def terms(values, degree):
        series = cheb.cheb2poly(cheb.chebfit(nodes, values, degree))
        out = np.zeros(1)
        for c in series[::-1]:
            out = poly.polyadd(poly.polymul(out, [-1.0, 8.0]), [c])
        return [float(np.float32(c)) for c in out[: degree + 1]]

    return terms(np.cos(2 * np.pi * r), 7), terms(np.sin(2 * np.pi * r) / r, 6)


COS_TERMS, SIN_TERMS = fit_terms()


def basis_table():
    centre = (np.arange(CHANNELS) - 0.5 * (CHANNELS - 1)) / CHANNELS
    columns = [np.ones_like(centre), centre, centre * centre]
    finished = []
    for column in columns:
        for before in finished:
            column = column - np.sum(column * before) * before
        finished.append(column / np.sqrt(np.sum(column * column)))
    return np.stack(finished, axis=1)


BASIS = basis_table()


def channel_weights(channel):
    centre = (np.arange(CHANNELS) - 0.5 * (CHANNELS - 1)) / CHANNELS
    square = centre * centre
    flat = BASIS[:, 0]
    lift = float(np.sum(square * flat))
    norm1 = float(np.sqrt(np.sum(centre * centre)))
    norm2 = float(np.sqrt(np.sum((square - lift * flat) ** 2)))
    x = (channel.astype(F32) - 0.5 * (CHANNELS - 1)) * (1.0 / CHANNELS)
    row = (float(flat[0]), x * (1.0 / norm1), (x * x - lift * float(flat[0])) * (1.0 / norm2))
    return [sum(row[j] * float(BASIS[f, j]) for j in range(3)) for f in range(CHANNELS)]


def horner(u, terms):
    out = jnp.full_like(u, terms[-1])
    for c in terms[-2::-1]:
        out = out * u + c
    return out


def wrapped(turns):
    return turns - jnp.round(turns)


def cos_turns(r):
    return horner(r * r, COS_TERMS)


def sin_turns(r):
    return r * horner(r * r, SIN_TERMS)


def split2(x):
    high = x.astype(BF16)
    return high, (x - high.astype(F32)).astype(BF16)


def split3(x):
    high = x.astype(BF16)
    rest = x - high.astype(F32)
    mid = rest.astype(BF16)
    return high, mid, (rest - mid.astype(F32)).astype(BF16)


def dot(a, b):
    return lax.dot_general(a, b, (((1,), (0,)), ((), ())), preferred_element_type=F32)


def dot_nt(a, b):
    return lax.dot_general(a, b, (((1,), (1,)), ((), ())), preferred_element_type=F32)


def chosen(pieces, table):
    return dot_nt(pieces[2], table) + dot_nt(pieces[1], table) + dot_nt(pieces[0], table)


def iota(shape, dim):
    return lax.broadcasted_iota(jnp.int32, shape, dim)


def as_table(cond):
    return jnp.where(cond, jnp.ones(cond.shape, F32), jnp.zeros(cond.shape, F32)).astype(BF16)


def station_at(place):
    inside = place & 127
    return ((inside >> 2) << 4) + ((place >> 7) << 2) + (inside & 3)


def packed(state):
    out = state[0:4, :]
    for a in range(1, 4):
        out = out + pltpu.roll(state, 32 * a, 1)[4 * a : 4 * a + 4, :]
    return out


def unpacked(tile):
    rows = [tile] + [pltpu.roll(tile, LANES - 32 * a, 1) for a in range(1, 4)]
    both = jnp.concatenate(rows, axis=0)
    return jnp.where(iota(both.shape, 1) < 2 * DIRS, both, 0.0)


def model_kernel(rows_ref, lmn_ref, flux_ref, map_ref, order_ref, model_ref, gains_ref, own_ref, table_ref, sky_ref, part_ref):
    first = lax.axis_index("stcol") * OWN
    scale = 1.0 + 0.5 * lax.axis_index("freq").astype(F32) / CHANNELS
    pieces = split3(rows_ref[...])
    place = station_at(iota((STATIONS, STATIONS), 0))
    moved = chosen(pieces, as_table(place == iota((STATIONS, STATIONS), 1)))
    gains_ref[...] = moved[0 : 2 * DIRS, :]
    table_ref[...] = as_table(place == order_ref[...])
    mine = as_table(iota((OWN, STATIONS), 1) == iota((OWN, STATIONS), 0) + first)
    own = sum(dot_nt(mine, piece) for piece in pieces[::-1])
    own = jnp.concatenate([own, jnp.zeros((OWN, LANES - own.shape[1]), F32)], axis=1)
    own_ref[...] = jnp.where(iota(own.shape, 1) < 2 * DIRS, own, 0.0)
    count = DIRS * SRC
    member = map_ref[...] == iota((DIRS, count), 0)
    member_f = jnp.where(member, 1.0, 0.0)
    blocks = count // LANES
    stacked = jnp.concatenate([member_f[:, b * LANES : (b + 1) * LANES] for b in range(blocks)], axis=0)
    ahead = as_table(iota((LANES, LANES), 0) <= iota((LANES, LANES), 1))
    running = dot(stacked.astype(BF16), ahead)
    carried = jnp.zeros((DIRS, 1), F32)
    ranks = []
    for b in range(blocks):
        here = running[b * DIRS : (b + 1) * DIRS, :] + carried
        ranks.append(jnp.sum(here * member_f[:, b * LANES : (b + 1) * LANES], axis=0, keepdims=True))
        carried = here[:, LANES - 1 : LANES]
    rank = jnp.concatenate(ranks, axis=1) - 1.0
    slots = as_table(iota((SRC, count), 0) == rank.astype(jnp.int32))
    values = [lmn_ref[0:1, :], lmn_ref[1:2, :], lmn_ref[2:3, :], flux_ref[...]]
    pieces = [[], [], []]
    for value in values:
        for s, piece in enumerate(split3(value)):
            pieces[s].append(piece.astype(F32) * member_f)
    pieces = [jnp.concatenate(p, axis=0).astype(BF16) for p in pieces]
    along = chosen(pieces, slots)
    down = dot_nt(slots, pieces[2]) + dot_nt(slots, pieces[1]) + dot_nt(slots, pieces[0])
    sky_ref[...] = jnp.concatenate([along, along], axis=1)
    part_ref[...] = down
    xyz = [scale * moved[2 * DIRS + c : 2 * DIRS + c + 1, :] for c in range(3)]
    own_xyz = [scale * own[:, 2 * DIRS + c : 2 * DIRS + c + 1] for c in range(3)]
    kept = station_at(iota((OWN, STATIONS), 1)) != iota((OWN, STATIONS), 0) + first
    half = iota((1, LANES), 1) < SRC
    shift_real = jnp.where(half, 0.0, 0.25)
    shift_imag = jnp.where(half, 0.25, 0.5)
    for k in range(DIRS):
        column = [part_ref[:, c * DIRS + k : c * DIRS + k + 1] for c in range(3)]
        turns = wrapped(xyz[0] * column[0] + xyz[1] * column[1] + xyz[2] * column[2])
        wave = jnp.concatenate([cos_turns(turns), sin_turns(turns)], axis=0)
        wave_high, wave_low = split2(wave)
        row = [sky_ref[c * DIRS + k : c * DIRS + k + 1, :] for c in range(4)]
        turns = wrapped(own_xyz[0] * row[0] + own_xyz[1] * row[1] + own_xyz[2] * row[2])
        near = jnp.concatenate([cos_turns(wrapped(turns - shift_real)), cos_turns(wrapped(turns - shift_imag))], axis=0)
        near_high, near_low = split2(near * row[3])
        model = dot(near_high, wave_low) + dot(near_low, wave_high) + dot(near_high, wave_high)
        model_ref[k, 0:OWN, :] = jnp.where(kept, model[0:OWN, :], 0.0)
        model_ref[k, OWN : 2 * OWN, :] = jnp.where(kept, model[OWN:, :], 0.0)


def one_pass(model_ref, vis_ref, gains, own, anchor, penalty, along_ref):
    pred_real = jnp.zeros((OWN, STATIONS), F32)
    pred_imag = jnp.zeros((OWN, STATIONS), F32)
    for k in range(DIRS):
        model_real = model_ref[k, 0:OWN, :]
        model_imag = model_ref[k, OWN : 2 * OWN, :]
        col_real = gains[k : k + 1, :]
        col_imag = gains[DIRS + k : DIRS + k + 1, :]
        along_real = model_real * col_real + model_imag * col_imag
        along_imag = model_imag * col_real - model_real * col_imag
        along_ref[k, 0:OWN, :] = along_real
        along_ref[k, OWN : 2 * OWN, :] = along_imag
        row_real = own[:, k : k + 1]
        row_imag = own[:, DIRS + k : DIRS + k + 1]
        pred_real = pred_real + (row_real * along_real - row_imag * along_imag)
        pred_imag = pred_imag + (row_real * along_imag + row_imag * along_real)
    resid_real = vis_ref[0:OWN, :] - pred_real
    resid_imag = vis_ref[OWN : 2 * OWN, :] - pred_imag
    lane = iota((OWN, LANES), 1)
    numer = jnp.zeros((OWN, LANES), F32)
    denom = jnp.zeros((OWN, LANES), F32)
    for k in range(DIRS):
        along_real = along_ref[k, 0:OWN, :]
        along_imag = along_ref[k, OWN : 2 * OWN, :]
        num_real = jnp.sum(resid_real * along_real + resid_imag * along_imag, axis=1, keepdims=True)
        num_imag = jnp.sum(resid_imag * along_real - resid_real * along_imag, axis=1, keepdims=True)
        den = jnp.sum(along_real * along_real + along_imag * along_imag, axis=1, keepdims=True)
        numer = jnp.where(lane == k, num_real, jnp.where(lane == DIRS + k, num_imag, numer))
        denom = jnp.where((lane == k) | (lane == DIRS + k), den, denom)
    fresh = (numer + own * denom + penalty * anchor) / (denom + penalty)
    return jnp.where(lane < 2 * DIRS, 0.5 * (own + fresh), 0.0)


def gathered_gains(tiles_ref):
    turned = jnp.transpose(tiles_ref[...])
    return jnp.concatenate([turned[32 * a : 32 * a + 32, :] for a in range(4)], axis=1)


def channel_fit(tiles_ref):
    weights = channel_weights(lax.axis_index("freq"))
    total = weights[0] * tiles_ref[0]
    for f in range(1, CHANNELS):
        total = total + weights[f] * tiles_ref[f]
    return unpacked(total)


def first_kernel(model_ref, tiles_ref, table_ref, gains_ref, own_ref, penalty_ref, vis_ref, state_ref, send_ref, along_ref):
    pieces = split3(gathered_gains(tiles_ref))
    vis_ref[...] = chosen(pieces, table_ref[...])
    own = own_ref[...]
    fresh = one_pass(model_ref, vis_ref, gains_ref[...], own, own, penalty_ref[...], along_ref)
    state_ref[...] = fresh
    send_ref[...] = packed(fresh)


def second_kernel(model_ref, vis_ref, tiles_ref, own_ref, anchor_ref, penalty_ref, state_ref, send_ref, along_ref):
    fresh = one_pass(model_ref, vis_ref, gathered_gains(tiles_ref), own_ref[...], anchor_ref[...], penalty_ref[...], along_ref)
    state_ref[...] = fresh
    send_ref[...] = packed(fresh)


def third_kernel(model_ref, vis_ref, tiles_ref, fit_ref, own_ref, penalty_ref, state_ref, anchor_ref, dual_ref, send_ref, along_ref):
    own = own_ref[...]
    cons = channel_fit(fit_ref)
    dual = own - cons
    anchor = cons - dual
    fresh = one_pass(model_ref, vis_ref, gathered_gains(tiles_ref), own, anchor, penalty_ref[...], along_ref)
    state_ref[...] = fresh
    anchor_ref[...] = anchor
    dual_ref[...] = dual
    send_ref[...] = packed(fresh)


def by_direction(state):
    filled = jnp.concatenate([state, jnp.zeros((LANES - OWN, LANES), F32)], axis=0)
    return jnp.transpose(filled)[0 : 2 * DIRS, 0:OWN]


def fourth_kernel(model_ref, vis_ref, tiles_ref, own_ref, anchor_ref, dual_ref, penalty_ref, out_ref, send_ref, along_ref):
    fresh = one_pass(model_ref, vis_ref, gathered_gains(tiles_ref), own_ref[...], anchor_ref[...], penalty_ref[...], along_ref)
    out_ref[...] = by_direction(fresh)
    send_ref[...] = packed(fresh + dual_ref[...])


def last_kernel(fit_ref, out_ref):
    out_ref[...] = by_direction(channel_fit(fit_ref))


def called(kernel, outs, scratch=(), name=None):
    return pl.pallas_call(
        kernel,
        out_shape=[jax.ShapeDtypeStruct(*o) for o in outs],
        scratch_shapes=list(scratch),
        compiler_params=pltpu.CompilerParams(vmem_limit_bytes=48 * 1024 * 1024),
        name=name,
    )


def exchanged(tile, axis):
    count = lax.axis_size(axis)
    tiles = lax.all_to_all(jnp.broadcast_to(tile, (count, *tile.shape)), axis, 0, 0, tiled=True)
    return tiles


def on_device(visibilities, positions, source_lmn, source_flux, cluster_map, station_order, penalty, offsets):
    tiles = visibilities.reshape(2, 4, 4, GROUP, OWN)
    tiles = tiles.transpose(3, 2, 1, 0, 4).reshape(GROUP, 4, LANES)
    tiles = lax.all_to_all(tiles, "stcol", 0, 0, tiled=True).reshape(LANES, LANES)
    order = station_order.reshape(GROUP, 4, 4).transpose(1, 0, 2).reshape(1, STATIONS)
    start = offsets.reshape(2, DIRS, STATIONS)
    rows = jnp.concatenate(
        [1.0 + start[0], start[1], positions.reshape(3, STATIONS), jnp.zeros((5, STATIONS), F32)], axis=0
    )
    pen = jnp.concatenate([penalty, penalty, jnp.ones((LANES - 2 * DIRS,), F32)]).reshape(1, LANES)
    model_out = ((DIRS, 2 * OWN, STATIONS), F32)
    state_out = ((OWN, LANES), F32)
    send_out = ((4, LANES), F32)
    flat_out = ((2 * DIRS, OWN), F32)
    along = pltpu.VMEM((DIRS, 2 * OWN, STATIONS), F32)
    model, gains, own, table = called(
        model_kernel,
        [model_out, ((2 * DIRS, STATIONS), F32), state_out, ((STATIONS, STATIONS), BF16)],
        [pltpu.VMEM((4 * DIRS, 2 * SRC), F32), pltpu.VMEM((SRC, 4 * DIRS), F32)],
        name="models",
    )(rows, source_lmn, source_flux.reshape(1, -1), cluster_map.reshape(1, -1), order)
    vis, state, send = called(
        first_kernel, [((2 * OWN, STATIONS), F32), state_out, send_out], [along], name="pass_one"
    )(model, tiles, table, gains, own, pen)
    got = exchanged(send, "stcol").reshape(LANES, LANES)
    state, send = called(second_kernel, [state_out, send_out], [along], name="pass_two")(
        model, vis, got, state, own, pen
    )
    got = exchanged(send, "stcol").reshape(LANES, LANES)
    fit = exchanged(send, "freq")
    state, anchor, dual, send = called(
        third_kernel, [state_out, state_out, state_out, send_out], [along], name="pass_three"
    )(model, vis, got, fit, state, pen)
    got = exchanged(send, "stcol").reshape(LANES, LANES)
    out, send = called(fourth_kernel, [flat_out, send_out], [along], name="pass_four")(
        model, vis, got, state, anchor, dual, pen
    )
    fit = exchanged(send, "freq")
    (cons,) = called(last_kernel, [flat_out], name="consensus")(fit)
    shape = (2, 1, DIRS, OWN)
    return out.reshape(shape), cons.reshape(shape)


def solution(mesh):
    in_specs = (
        P(None, "freq", "stcol", None, None),
        P(),
        P(),
        P(),
        P(),
        P(),
        P(),
        P(None, "freq", None, None),
    )
    out_specs = (P(None, "freq", None, "stcol"), P(None, "freq", None, "stcol"))
    return jax.shard_map(
        on_device, mesh=mesh, in_specs=in_specs, out_specs=out_specs, check_vma=False
    )
```

```python
import math

import jax
import jax.numpy as jnp
import numpy as np
from jax import lax
from jax.experimental import pallas as pl
from jax.experimental.pallas import tpu as pltpu
from jax.sharding import PartitionSpec as P

STATIONS = 512
DIRS = 16
SRC = 64
CHANNELS = 8
OWN = 16
REPS = 2
ROWS = REPS * OWN
MEMBERS = STATIONS // ROWS
LANES = 128
F32 = jnp.float32
BF16 = jnp.bfloat16

COS_TERMS = None
SIN_TERMS = None


def fit_terms():
    nodes = np.cos(np.pi * (np.arange(400) + 0.5) / 400)
    u = 0.125 * (nodes + 1.0)
    r = np.sqrt(u)
    cheb = np.polynomial.chebyshev
    poly = np.polynomial.polynomial

    def terms(values, degree):
        series = cheb.cheb2poly(cheb.chebfit(nodes, values, degree))
        out = np.zeros(1)
        for c in series[::-1]:
            out = poly.polyadd(poly.polymul(out, [-1.0, 8.0]), [c])
        return [float(np.float32(c)) for c in out[: degree + 1]]

    return terms(np.cos(2 * np.pi * r), 7), terms(np.sin(2 * np.pi * r) / r, 6)


COS_TERMS, SIN_TERMS = fit_terms()


def basis_table():
    centre = (np.arange(CHANNELS) - 0.5 * (CHANNELS - 1)) / CHANNELS
    columns = [np.ones_like(centre), centre, centre * centre]
    finished = []
    for column in columns:
        for before in finished:
            column = column - np.sum(column * before) * before
        finished.append(column / np.sqrt(np.sum(column * column)))
    return np.stack(finished, axis=1)


BASIS = basis_table()


def basis_row(channel):
    centre = (np.arange(CHANNELS) - 0.5 * (CHANNELS - 1)) / CHANNELS
    square = centre * centre
    flat = BASIS[:, 0]
    lift = float(np.sum(square * flat))
    norm1 = float(np.sqrt(np.sum(centre * centre)))
    norm2 = float(np.sqrt(np.sum((square - lift * flat) ** 2)))
    x = (channel.astype(F32) - 0.5 * (CHANNELS - 1)) * (1.0 / CHANNELS)
    return (float(flat[0]), x * (1.0 / norm1), (x * x - lift * float(flat[0])) * (1.0 / norm2))


def channel_weights(channel):
    row = basis_row(channel)
    return [sum(row[j] * float(BASIS[f, j]) for j in range(3)) for f in range(CHANNELS)]


def channel_weight(channel, source):
    return sum(a * b for a, b in zip(basis_row(channel), basis_row(source)))


def horner(u, terms):
    out = jnp.full_like(u, terms[-1])
    for c in terms[-2::-1]:
        out = out * u + c
    return out


def wrapped(turns):
    return turns - jnp.round(turns)


def cos_turns(r):
    return horner(r * r, COS_TERMS)


def sin_turns(r):
    return r * horner(r * r, SIN_TERMS)


def split2(x):
    high = x.astype(BF16)
    return high, (x - high.astype(F32)).astype(BF16)


def split3(x):
    high = x.astype(BF16)
    rest = x - high.astype(F32)
    mid = rest.astype(BF16)
    return high, mid, (rest - mid.astype(F32)).astype(BF16)


def dot(a, b):
    return lax.dot_general(a, b, (((1,), (0,)), ((), ())), preferred_element_type=F32)


def dot_nt(a, b):
    return lax.dot_general(a, b, (((1,), (1,)), ((), ())), preferred_element_type=F32)


def chosen(pieces, table):
    return dot_nt(pieces[2], table) + dot_nt(pieces[1], table) + dot_nt(pieces[0], table)


def iota(shape, dim):
    return lax.broadcasted_iota(jnp.int32, shape, dim)


def as_table(cond):
    return jnp.where(cond, jnp.ones(cond.shape, F32), jnp.zeros(cond.shape, F32)).astype(BF16)


def station_at(place):
    member = (place >> 3) & 15
    return ((member >> 2) << 7) + ((place >> 8) << 6) + ((member & 3) << 4) + (((place >> 7) & 1) << 3) + (place & 7)


def row_station(shape, dim, device):
    row = iota(shape, dim)
    return ((row >> 4) << 6) + (row & 15) + ((device >> 3) << 7) + ((device & 3) << 4)


def rep_of(device):
    return (device & 7) >> 2


def packed(state):
    n = state.shape[0] // 4
    out = state[0:n, :]
    for a in range(1, 4):
        out = out + pltpu.roll(state, 32 * a, 1)[n * a : n * a + n, :]
    return out


def unpacked(tile):
    rows = [tile] + [pltpu.roll(tile, LANES - 32 * a, 1) for a in range(1, 4)]
    both = jnp.concatenate(rows, axis=0)
    return jnp.where(iota(both.shape, 1) < 2 * DIRS, both, 0.0)


def turn_kernel(vis_hbm, tiles_ref, vis_ref, sem):
    copy = pltpu.make_async_copy(vis_hbm, vis_ref, sem)
    copy.start()
    copy.wait()
    lane = iota((8, LANES), 1)
    for x in range(4):
        parts = [vis_ref[r * 8 : (r + 1) * 8, 0, x * LANES : (x + 1) * LANES] for r in range(4)]
        for b in range(4):
            tile = jnp.zeros((8, LANES), F32)
            for half in range(2):
                for r in range(2):
                    for a in range(REPS):
                        to = half * 64 + r * ROWS + a * OWN
                        moved = pltpu.roll(parts[2 * r + half], (to - (64 * a + 16 * b)) % LANES, 1)
                        tile = jnp.where((lane >> 4) == (to >> 4), moved, tile)
            for a in range(REPS):
                tiles_ref[x * 8 + 4 * a + b] = tile


def products(model_ref, gains_ref, start, k):
    half = model_ref.shape[1] // 2
    model_real = model_ref[k, pl.ds(start, OWN), :]
    model_imag = model_ref[k, pl.ds(start + half, OWN), :]
    col_real = gains_ref[k : k + 1, :]
    col_imag = gains_ref[DIRS + k : DIRS + k + 1, :]
    return model_real * col_real + model_imag * col_imag, model_imag * col_real - model_real * col_imag


def predict(model_ref, gains_ref, own, start, along_ref):
    pred_real = jnp.zeros((OWN, STATIONS), F32)
    pred_imag = jnp.zeros((OWN, STATIONS), F32)
    lane = iota((OWN, LANES), 1)
    denom = jnp.zeros((OWN, LANES), F32)
    for k in range(DIRS):
        along_real, along_imag = products(model_ref, gains_ref, start, k)
        if along_ref is not None:
            along_ref[k, 0:OWN, :] = along_real
            along_ref[k, OWN : 2 * OWN, :] = along_imag
        row_real = own[:, k : k + 1]
        row_imag = own[:, DIRS + k : DIRS + k + 1]
        pred_real = pred_real + (row_real * along_real - row_imag * along_imag)
        pred_imag = pred_imag + (row_real * along_imag + row_imag * along_real)
        den = jnp.sum(along_real * along_real + along_imag * along_imag, axis=1, keepdims=True)
        denom = jnp.where((lane == k) | (lane == DIRS + k), den, denom)
    return pred_real, pred_imag, denom


def correlate(resid_real, resid_imag, along):
    lane = iota((OWN, LANES), 1)
    numer = jnp.zeros((OWN, LANES), F32)
    for k in range(DIRS):
        along_real, along_imag = along(k)
        num_real = jnp.sum(resid_real * along_real + resid_imag * along_imag, axis=1, keepdims=True)
        num_imag = jnp.sum(resid_imag * along_real - resid_real * along_imag, axis=1, keepdims=True)
        numer = jnp.where(lane == k, num_real, jnp.where(lane == DIRS + k, num_imag, numer))
    return numer


def row_sums(model_ref, vis_ref, gains_ref, own, start, along_ref):
    pred_real, pred_imag, denom = predict(model_ref, gains_ref, own, start, along_ref)
    resid_real = vis_ref[pl.ds(start, OWN), :] - pred_real
    resid_imag = vis_ref[pl.ds(start + ROWS, OWN), :] - pred_imag
    numer = correlate(resid_real, resid_imag, lambda k: (along_ref[k, 0:OWN, :], along_ref[k, OWN : 2 * OWN, :]))
    return numer, denom


def updated(numer, denom, own, anchor, penalty):
    fresh = (numer + own * denom + penalty * anchor) / (denom + penalty)
    return jnp.where(iota(own.shape, 1) < 2 * DIRS, 0.5 * (own + fresh), 0.0)


def model_kernel(
    offs_hbm, place_hbm, lmn_hbm, flux_hbm, map_hbm, order_ref, penalty_hbm,
    model_ref, own_ref, table_ref, gains_ref, pred_ref, den_ref, weight_ref,
    offs_ref, xyz_ref, lmn_ref, flux_ref, map_ref, penalty_ref, sky_ref, part_ref, sems,
):
    pairs = [
        (map_hbm, map_ref), (lmn_hbm, lmn_ref), (flux_hbm, flux_ref),
        (offs_hbm, offs_ref), (place_hbm, xyz_ref), (penalty_hbm, penalty_ref),
    ]
    copies = [pltpu.make_async_copy(a, b, sems.at[n]) for n, (a, b) in enumerate(pairs)]
    for copy in copies:
        copy.start()
    device = lax.axis_index("stcol")
    scale = 1.0 + 0.5 * lax.axis_index("freq").astype(F32) / CHANNELS
    for copy in copies:
        copy.wait()
    lane = iota((1, LANES), 1)
    weight = jnp.ones((1, LANES), F32)
    for k in range(DIRS):
        weight = jnp.where((lane == k) | (lane == DIRS + k), penalty_ref[0, k], weight)
    weight_ref[...] = weight
    offs = offs_ref[...]
    rows = [1.0 + offs[0:DIRS, :], offs[DIRS : 2 * DIRS, :]] + [xyz_ref[c] for c in range(3)]
    pieces = split3(jnp.concatenate(rows + [jnp.zeros((5, STATIONS), F32)], axis=0))
    place = station_at(iota((STATIONS, STATIONS), 0))
    moved = chosen(pieces, as_table(place == iota((STATIONS, STATIONS), 1)))
    gains_ref[...] = moved[0 : 2 * DIRS, :]
    table_ref[...] = as_table(place == order_ref[...])
    mine = as_table(iota((ROWS, STATIONS), 1) == row_station((ROWS, STATIONS), 0, device))
    own = sum(dot_nt(mine, piece) for piece in pieces[::-1])
    own = jnp.concatenate([own, jnp.zeros((ROWS, LANES - own.shape[1]), F32)], axis=1)
    own_xyz = [scale * own[:, 2 * DIRS + c : 2 * DIRS + c + 1] for c in range(3)]
    own_ref[...] = jnp.where(iota(own.shape, 1) < 2 * DIRS, own, 0.0)
    count = DIRS * SRC
    member = map_ref[...] == iota((DIRS, count), 0)
    member_f = jnp.where(member, 1.0, 0.0)
    blocks = count // LANES
    stacked = jnp.concatenate([member_f[:, b * LANES : (b + 1) * LANES] for b in range(blocks)], axis=0)
    ahead = as_table(iota((LANES, LANES), 0) <= iota((LANES, LANES), 1))
    running = dot(stacked.astype(BF16), ahead)
    carried = jnp.zeros((DIRS, 1), F32)
    ranks = []
    for b in range(blocks):
        here = running[b * DIRS : (b + 1) * DIRS, :] + carried
        ranks.append(jnp.sum(here * member_f[:, b * LANES : (b + 1) * LANES], axis=0, keepdims=True))
        carried = here[:, LANES - 1 : LANES]
    rank = jnp.concatenate(ranks, axis=1) - 1.0
    slots = as_table(iota((SRC, count), 0) == rank.astype(jnp.int32))
    values = [lmn_ref[0:1, :], lmn_ref[1:2, :], lmn_ref[2:3, :], flux_ref[...]]
    pieces = [[], [], []]
    for value in values:
        for s, piece in enumerate(split3(value)):
            pieces[s].append(piece.astype(F32) * member_f)
    pieces = [jnp.concatenate(p, axis=0).astype(BF16) for p in pieces]
    along = chosen(pieces, slots)
    down = dot_nt(slots, pieces[2]) + dot_nt(slots, pieces[1]) + dot_nt(slots, pieces[0])
    sky_ref[...] = jnp.concatenate([along, along], axis=1)
    part_ref[...] = down
    xyz = [scale * moved[2 * DIRS + c : 2 * DIRS + c + 1, :] for c in range(3)]
    kept = station_at(iota((ROWS, STATIONS), 1)) != row_station((ROWS, STATIONS), 0, device)
    half = iota((1, LANES), 1) < SRC
    shift_real = jnp.where(half, 0.0, 0.25)
    shift_imag = jnp.where(half, 0.25, 0.5)
    for k in range(DIRS):
        column = [part_ref[:, c * DIRS + k : c * DIRS + k + 1] for c in range(3)]
        turns = wrapped(xyz[0] * column[0] + xyz[1] * column[1] + xyz[2] * column[2])
        wave = jnp.concatenate([cos_turns(turns), sin_turns(turns)], axis=0)
        wave_high, wave_low = split2(wave)
        row = [sky_ref[c * DIRS + k : c * DIRS + k + 1, :] for c in range(4)]
        turns = wrapped(own_xyz[0] * row[0] + own_xyz[1] * row[1] + own_xyz[2] * row[2])
        near = jnp.concatenate([cos_turns(wrapped(turns - shift_real)), cos_turns(wrapped(turns - shift_imag))], axis=0)
        near_high, near_low = split2(near * row[3])
        model = dot(near_high, wave_low) + dot(near_low, wave_high) + dot(near_high, wave_high)
        model_ref[k, 0:ROWS, :] = jnp.where(kept, model[0:ROWS, :], 0.0)
        model_ref[k, ROWS : 2 * ROWS, :] = jnp.where(kept, model[ROWS:, :], 0.0)
    for a in range(REPS):
        rows = slice(a * OWN, (a + 1) * OWN)
        pred_real, pred_imag, denom = predict(model_ref, gains_ref, own_ref[rows, :], a * OWN, None)
        pred_ref[rows, :] = pred_real
        pred_ref[ROWS + a * OWN : ROWS + (a + 1) * OWN, :] = pred_imag
        den_ref[rows, :] = denom


def gathered_gains(tiles_ref):
    turned = jnp.transpose(tiles_ref[...])
    return jnp.concatenate([turned[32 * a : 32 * a + 32, :] for a in range(4)], axis=1)


def channel_fit(tiles_ref):
    weights = channel_weights(lax.axis_index("freq"))
    total = weights[0] * tiles_ref[0]
    for f in range(1, CHANNELS):
        total = total + weights[f] * tiles_ref[f]
    return total


def sums(model_ref, vis_ref, tiles_ref, own_ref, numer_ref, den_ref, along_ref, gains_ref):
    gains_ref[...] = gathered_gains(tiles_ref)
    for a in range(REPS):
        rows = slice(a * OWN, (a + 1) * OWN)
        numer, denom = row_sums(model_ref, vis_ref, gains_ref, own_ref[rows, :], a * OWN, along_ref)
        numer_ref[rows, :] = numer
        den_ref[rows, :] = denom


def first_kernel(tiles_ref, table_ref, model_ref, gains_ref, pred_ref, den_ref, own_ref, penalty_ref, vis_ref, state_ref, send_ref):
    turned = jnp.transpose(tiles_ref[...])
    pieces = split3(jnp.concatenate([turned[0 : 2 * ROWS, :], turned[2 * ROWS :, :]], axis=1))
    vis_ref[...] = chosen(pieces, table_ref[...])
    for a in range(REPS):
        rows = slice(a * OWN, (a + 1) * OWN)
        lower = slice(ROWS + a * OWN, ROWS + (a + 1) * OWN)
        resid_real = vis_ref[rows, :] - pred_ref[rows, :]
        resid_imag = vis_ref[lower, :] - pred_ref[lower, :]
        numer = correlate(resid_real, resid_imag, lambda k: products(model_ref, gains_ref, a * OWN, k))
        own = own_ref[rows, :]
        state_ref[rows, :] = updated(numer, den_ref[rows, :], own, own, penalty_ref[...])
    send_ref[...] = packed(state_ref[...])


def second_kernel(
    model_ref, vis_ref, tiles_ref, own_ref, anchor_ref, penalty_ref, state_ref, send_ref, along_ref, gains_ref, den_ref
):
    sums(model_ref, vis_ref, tiles_ref, own_ref, state_ref, den_ref, along_ref, gains_ref)
    state = updated(state_ref[...], den_ref[...], own_ref[...], anchor_ref[...], penalty_ref[...])
    state_ref[...] = state
    send_ref[...] = packed(state)


def anchor_kernel(numer_ref, den_ref, near_ref, far_ref, own_ref, penalty_ref, state_ref, anchor_ref, dual_ref, send_ref):
    own = own_ref[...]
    channel = lax.axis_index("freq")
    total = None
    for d in range(CHANNELS // 2):
        other = (channel - 2 * d) & (CHANNELS - 1)
        for tiles_ref, source in ((near_ref, other), (far_ref, other ^ 1)):
            part = channel_weight(channel, source) * tiles_ref[d]
            total = part if total is None else total + part
    cons = unpacked(total)
    dual = own - cons
    anchor = cons - dual
    state = updated(numer_ref[...], den_ref[...], own, anchor, penalty_ref[...])
    state_ref[...] = state
    send_ref[...] = packed(state)
    anchor_ref[...] = anchor
    dual_ref[...] = dual


def by_direction(state):
    filled = jnp.concatenate([state, jnp.zeros((LANES - OWN, LANES), F32)], axis=0)
    return jnp.transpose(filled)[0 : 2 * DIRS, 0:OWN]


def fourth_kernel(
    model_ref, vis_ref, tiles_ref, own_ref, anchor_ref, dual_ref, penalty_ref, state_ref, send_ref, along_ref, gains_ref
):
    start = pl.multiple_of(rep_of(lax.axis_index("stcol")) * OWN, OWN)
    rows = pl.ds(start, OWN)
    own = own_ref[rows, :]
    gains_ref[...] = gathered_gains(tiles_ref)
    numer, denom = row_sums(model_ref, vis_ref, gains_ref, own, start, along_ref)
    state = updated(numer, denom, own, anchor_ref[rows, :], penalty_ref[...])
    state_ref[...] = state
    send_ref[...] = packed(state + dual_ref[rows, :])


def last_kernel(fit_ref, state_ref, out_ref, cons_ref):
    out_ref[...] = by_direction(state_ref[...])
    cons_ref[...] = by_direction(unpacked(channel_fit(fit_ref)))


def called(kernel, outs, scratch=(), name=None, in_specs=None):
    return pl.pallas_call(
        kernel,
        out_shape=[jax.ShapeDtypeStruct(*o) for o in outs],
        scratch_shapes=[pltpu.VMEM(*o) if isinstance(o, tuple) else o for o in scratch],
        compiler_params=pltpu.CompilerParams(vmem_limit_bytes=32 * 1024 * 1024),
        name=name,
        **({} if in_specs is None else {"in_specs": in_specs}),
    )


def held(x):
    return pltpu.with_memory_space_constraint(x, pltpu.HBM)


def to_all(tile, axis, count, groups=None):
    tiles = jnp.broadcast_to(tile, (count, *tile.shape))
    return lax.all_to_all(tiles, axis, 0, 0, tiled=True, axis_index_groups=groups)


def to_members(tile):
    groups = [[x * 8 + 4 * m + b for x in range(4) for b in range(4)] for m in range(REPS)]
    return to_all(tile, "stcol", MEMBERS, groups).reshape(LANES, LANES)


def on_device(visibilities, positions, source_lmn, source_flux, cluster_map, station_order, penalty, offsets):
    hbm = pl.BlockSpec(memory_space=pltpu.HBM)
    vmem = pl.BlockSpec(memory_space=pltpu.VMEM)
    model_out = ((DIRS, 2 * ROWS, STATIONS), F32)
    along = ((DIRS, 2 * OWN, STATIONS), F32)
    vis_out = ((2 * ROWS, STATIONS), F32)
    state_out = ((ROWS, LANES), F32)
    send_out = ((ROWS // 4, LANES), F32)
    flat_out = ((2 * DIRS, OWN), F32)
    gains_out = ((2 * DIRS, STATIONS), F32)
    (tiles,) = called(
        turn_kernel,
        [((STATIONS // OWN, 8, LANES), F32)],
        [((2 * OWN, 1, STATIONS), F32), pltpu.SemaphoreType.DMA],
        "turn",
        [hbm],
    )(held(visibilities.reshape(2 * OWN, 1, STATIONS)))
    tiles = lax.all_to_all(tiles, "stcol", 0, 0, tiled=True).reshape(STATIONS // 2, LANES)
    order = station_order.reshape(STATIONS // OWN, 2, 8).transpose(1, 0, 2).reshape(1, STATIONS)
    count = DIRS * SRC
    model, own, table, gains, pred, den, pen = called(
        model_kernel,
        [model_out, state_out, ((STATIONS, STATIONS), BF16), gains_out, vis_out, state_out, ((1, LANES), F32)],
        [
            gains_out, ((3, 1, STATIONS), F32), ((3, count), F32), ((1, count), F32), ((1, count), jnp.int32),
            pltpu.SMEM((1, DIRS), F32), ((4 * DIRS, 2 * SRC), F32), ((SRC, 4 * DIRS), F32),
            pltpu.SemaphoreType.DMA((6,)),
        ],
        "models",
        [hbm, hbm, hbm, hbm, hbm, vmem, hbm],
    )(
        held(offsets.reshape(2 * DIRS, STATIONS)), held(positions), held(source_lmn), held(source_flux.reshape(1, count)),
        held(cluster_map.reshape(1, count)), order, held(penalty.reshape(1, DIRS)),
    )
    vis, state, send = called(first_kernel, [vis_out, state_out, send_out], name="pass_one")(
        tiles, table, model, gains, pred, den, own, pen
    )
    got = to_members(send)
    state, send = called(second_kernel, [state_out, send_out], [along, gains_out, state_out], "pass_two")(
        model, vis, got, state, own, pen
    )
    near = [send] + [
        lax.ppermute(send, "freq", [(i, (i + 2 * d) % CHANNELS) for i in range(CHANNELS)]) for d in range(1, CHANNELS // 2)
    ]
    near = jnp.stack(near)
    far = lax.ppermute(near, "freq", [(i, i ^ 1) for i in range(CHANNELS)])
    got = to_members(send)
    numer, den = called(sums, [state_out, state_out], [along, gains_out], "pass_three")(model, vis, got, state)
    state, anchor, dual, send = called(anchor_kernel, [state_out, state_out, state_out, send_out], name="update_three")(
        numer, den, near, far, state, pen
    )
    got = to_members(send)
    state, send = called(fourth_kernel, [((OWN, LANES), F32), ((4, LANES), F32)], [along, gains_out], "pass_four")(
        model, vis, got, state, anchor, dual, pen
    )
    out, cons = called(last_kernel, [flat_out, flat_out], name="consensus")(to_all(send, "freq", CHANNELS), state)
    shape = (2, 1, DIRS, OWN)
    return out.reshape(shape), cons.reshape(shape)


def solution(mesh):
    in_specs = (
        P(None, "freq", "stcol", None, None),
        P(),
        P(),
        P(),
        P(),
        P(),
        P(),
        P(None, "freq", None, None),
    )
    out_specs = (P(None, "freq", None, "stcol"), P(None, "freq", None, "stcol"))
    return jax.shard_map(
        on_device, mesh=mesh, in_specs=in_specs, out_specs=out_specs, check_vma=False
    )
```

```python
import math

import jax
import jax.numpy as jnp
import numpy as np
from jax import lax
from jax.experimental import pallas as pl
from jax.experimental.pallas import tpu as pltpu
from jax.sharding import PartitionSpec as P

STATIONS = 512
DIRS = 16
SRC = 64
CHANNELS = 8
OWN = 16
REPS = 2
ROWS = REPS * OWN
MEMBERS = STATIONS // ROWS
LANES = 128
FRONT = 10
LEAD = 31
F32 = jnp.float32
BF16 = jnp.bfloat16

COS_TERMS = None
SIN_TERMS = None


def fit_terms():
    nodes = np.cos(np.pi * (np.arange(400) + 0.5) / 400)
    u = 0.125 * (nodes + 1.0)
    r = np.sqrt(u)
    cheb = np.polynomial.chebyshev
    poly = np.polynomial.polynomial

    def terms(values, degree):
        series = cheb.cheb2poly(cheb.chebfit(nodes, values, degree))
        out = np.zeros(1)
        for c in series[::-1]:
            out = poly.polyadd(poly.polymul(out, [-1.0, 8.0]), [c])
        return [float(np.float32(c)) for c in out[: degree + 1]]

    return terms(np.cos(2 * np.pi * r), 7), terms(np.sin(2 * np.pi * r) / r, 6)


COS_TERMS, SIN_TERMS = fit_terms()


def basis_table():
    centre = (np.arange(CHANNELS) - 0.5 * (CHANNELS - 1)) / CHANNELS
    columns = [np.ones_like(centre), centre, centre * centre]
    finished = []
    for column in columns:
        for before in finished:
            column = column - np.sum(column * before) * before
        finished.append(column / np.sqrt(np.sum(column * column)))
    return np.stack(finished, axis=1)


BASIS = basis_table()


def basis_row(channel):
    centre = (np.arange(CHANNELS) - 0.5 * (CHANNELS - 1)) / CHANNELS
    square = centre * centre
    flat = BASIS[:, 0]
    lift = float(np.sum(square * flat))
    norm1 = float(np.sqrt(np.sum(centre * centre)))
    norm2 = float(np.sqrt(np.sum((square - lift * flat) ** 2)))
    x = (channel.astype(F32) - 0.5 * (CHANNELS - 1)) * (1.0 / CHANNELS)
    return (float(flat[0]), x * (1.0 / norm1), (x * x - lift * float(flat[0])) * (1.0 / norm2))


def channel_weight(channel, source):
    return sum(a * b for a, b in zip(basis_row(channel), basis_row(source)))


def basis_product(channel, source):
    return sum(a * float(b) for a, b in zip(basis_row(channel), BASIS[source]))


def horner(u, terms):
    out = jnp.full_like(u, terms[-1])
    for c in terms[-2::-1]:
        out = out * u + c
    return out


def wrapped(turns):
    return turns - jnp.round(turns)


def cos_turns(r):
    return horner(r * r, COS_TERMS)


def sin_turns(r):
    return r * horner(r * r, SIN_TERMS)


def split2(x):
    high = x.astype(BF16)
    return high, (x - high.astype(F32)).astype(BF16)


def split3(x):
    high = x.astype(BF16)
    rest = x - high.astype(F32)
    mid = rest.astype(BF16)
    return high, mid, (rest - mid.astype(F32)).astype(BF16)


def dot(a, b):
    return lax.dot_general(a, b, (((1,), (0,)), ((), ())), preferred_element_type=F32)


def dot_nt(a, b):
    return lax.dot_general(a, b, (((1,), (1,)), ((), ())), preferred_element_type=F32)


def chosen(pieces, table):
    return dot_nt(pieces[2], table) + dot_nt(pieces[1], table) + dot_nt(pieces[0], table)


def iota(shape, dim):
    return lax.broadcasted_iota(jnp.int32, shape, dim)


def as_table(cond):
    return jnp.where(cond, jnp.ones(cond.shape, F32), jnp.zeros(cond.shape, F32)).astype(BF16)


def station_at(place):
    member = ((place >> 3) & 15) ^ FRONT
    return ((member >> 2) << 7) + ((place >> 8) << 6) + ((member & 3) << 4) + (((place >> 7) & 1) << 3) + (place & 7)


def row_station(shape, dim, device):
    row = iota(shape, dim)
    return ((row >> 4) << 6) + (row & 15) + ((device >> 3) << 7) + ((device & 3) << 4)


def rep_of(device):
    return (device & 7) >> 2


def packed(state):
    n = state.shape[0] // 4
    out = state[0:n, :]
    for a in range(1, 4):
        out = out + pltpu.roll(state, 32 * a, 1)[n * a : n * a + n, :]
    return out


def unpacked(tile):
    rows = [tile] + [pltpu.roll(tile, LANES - 32 * a, 1) for a in range(1, 4)]
    both = jnp.concatenate(rows, axis=0)
    return jnp.where(iota(both.shape, 1) < 2 * DIRS, both, 0.0)


def turn_kernel(vis_hbm, tiles_ref, vis_ref, sem):
    copy = pltpu.make_async_copy(vis_hbm, vis_ref, sem)
    copy.start()
    copy.wait()
    lane = iota((8, LANES), 1)
    for x in range(4):
        parts = [vis_ref[r * 8 : (r + 1) * 8, 0, x * LANES : (x + 1) * LANES] for r in range(4)]
        for b in range(4):
            tile = jnp.zeros((8, LANES), F32)
            for half in range(2):
                for r in range(2):
                    for a in range(REPS):
                        to = half * 64 + r * ROWS + a * OWN
                        moved = pltpu.roll(parts[2 * r + half], (to - (64 * a + 16 * b)) % LANES, 1)
                        tile = jnp.where((lane >> 4) == (to >> 4), moved, tile)
            for a in range(REPS):
                tiles_ref[(x * 8 + 4 * a + b) ^ LEAD] = tile


def products(model_ref, gains_ref, start, k):
    half = model_ref.shape[1] // 2
    model_real = model_ref[k, pl.ds(start, OWN), :]
    model_imag = model_ref[k, pl.ds(start + half, OWN), :]
    col_real = gains_ref[k : k + 1, :]
    col_imag = gains_ref[DIRS + k : DIRS + k + 1, :]
    return model_real * col_real + model_imag * col_imag, model_imag * col_real - model_real * col_imag


def predict(model_ref, gains_ref, own, start, along_ref):
    pred_real = jnp.zeros((OWN, STATIONS), F32)
    pred_imag = jnp.zeros((OWN, STATIONS), F32)
    lane = iota((OWN, LANES), 1)
    denom = jnp.zeros((OWN, LANES), F32)
    for k in range(DIRS):
        along_real, along_imag = products(model_ref, gains_ref, start, k)
        if along_ref is not None:
            along_ref[k, 0:OWN, :] = along_real
            along_ref[k, OWN : 2 * OWN, :] = along_imag
        row_real = own[:, k : k + 1]
        row_imag = own[:, DIRS + k : DIRS + k + 1]
        pred_real = pred_real + (row_real * along_real - row_imag * along_imag)
        pred_imag = pred_imag + (row_real * along_imag + row_imag * along_real)
        den = jnp.sum(along_real * along_real + along_imag * along_imag, axis=1, keepdims=True)
        denom = jnp.where((lane == k) | (lane == DIRS + k), den, denom)
    return pred_real, pred_imag, denom


def correlate(resid_real, resid_imag, along):
    lane = iota((OWN, LANES), 1)
    numer = jnp.zeros((OWN, LANES), F32)
    for k in range(DIRS):
        along_real, along_imag = along(k)
        num_real = jnp.sum(resid_real * along_real + resid_imag * along_imag, axis=1, keepdims=True)
        num_imag = jnp.sum(resid_imag * along_real - resid_real * along_imag, axis=1, keepdims=True)
        numer = jnp.where(lane == k, num_real, jnp.where(lane == DIRS + k, num_imag, numer))
    return numer


def row_sums(model_ref, vis_ref, gains_ref, own, start, along_ref):
    pred_real, pred_imag, denom = predict(model_ref, gains_ref, own, start, along_ref)
    resid_real = vis_ref[pl.ds(start, OWN), :] - pred_real
    resid_imag = vis_ref[pl.ds(start + ROWS, OWN), :] - pred_imag
    numer = correlate(resid_real, resid_imag, lambda k: (along_ref[k, 0:OWN, :], along_ref[k, OWN : 2 * OWN, :]))
    return numer, denom


def updated(numer, denom, own, anchor, penalty):
    fresh = (numer + own * denom + penalty * anchor) / (denom + penalty)
    return jnp.where(iota(own.shape, 1) < 2 * DIRS, 0.5 * (own + fresh), 0.0)


def model_kernel(
    offs_hbm, place_hbm, lmn_hbm, flux_hbm, map_hbm, order_ref, penalty_hbm,
    model_ref, own_ref, table_ref, gains_ref, pred_ref, den_ref, weight_ref,
    offs_ref, xyz_ref, lmn_ref, flux_ref, map_ref, penalty_ref, sky_ref, part_ref, sems,
):
    pairs = [
        (map_hbm, map_ref), (lmn_hbm, lmn_ref), (flux_hbm, flux_ref),
        (offs_hbm, offs_ref), (place_hbm, xyz_ref), (penalty_hbm, penalty_ref),
    ]
    copies = [pltpu.make_async_copy(a, b, sems.at[n]) for n, (a, b) in enumerate(pairs)]
    for copy in copies:
        copy.start()
    device = lax.axis_index("stcol")
    scale = 1.0 + 0.5 * lax.axis_index("freq").astype(F32) / CHANNELS
    for copy in copies:
        copy.wait()
    lane = iota((1, LANES), 1)
    weight = jnp.ones((1, LANES), F32)
    for k in range(DIRS):
        weight = jnp.where((lane == k) | (lane == DIRS + k), penalty_ref[0, k], weight)
    weight_ref[...] = weight
    offs = offs_ref[...]
    rows = [1.0 + offs[0:DIRS, :], offs[DIRS : 2 * DIRS, :]] + [xyz_ref[c] for c in range(3)]
    pieces = split3(jnp.concatenate(rows + [jnp.zeros((5, STATIONS), F32)], axis=0))
    place = station_at(iota((STATIONS, STATIONS), 0))
    moved = chosen(pieces, as_table(place == iota((STATIONS, STATIONS), 1)))
    gains_ref[...] = moved[0 : 2 * DIRS, :]
    table_ref[...] = as_table(place == order_ref[...])
    mine = as_table(iota((ROWS, STATIONS), 1) == row_station((ROWS, STATIONS), 0, device))
    own = sum(dot_nt(mine, piece) for piece in pieces[::-1])
    own = jnp.concatenate([own, jnp.zeros((ROWS, LANES - own.shape[1]), F32)], axis=1)
    own_xyz = [scale * own[:, 2 * DIRS + c : 2 * DIRS + c + 1] for c in range(3)]
    own_ref[...] = jnp.where(iota(own.shape, 1) < 2 * DIRS, own, 0.0)
    count = DIRS * SRC
    member = map_ref[...] == iota((DIRS, count), 0)
    member_f = jnp.where(member, 1.0, 0.0)
    blocks = count // LANES
    stacked = jnp.concatenate([member_f[:, b * LANES : (b + 1) * LANES] for b in range(blocks)], axis=0)
    ahead = as_table(iota((LANES, LANES), 0) <= iota((LANES, LANES), 1))
    running = dot(stacked.astype(BF16), ahead)
    carried = jnp.zeros((DIRS, 1), F32)
    ranks = []
    for b in range(blocks):
        here = running[b * DIRS : (b + 1) * DIRS, :] + carried
        ranks.append(jnp.sum(here * member_f[:, b * LANES : (b + 1) * LANES], axis=0, keepdims=True))
        carried = here[:, LANES - 1 : LANES]
    rank = jnp.concatenate(ranks, axis=1) - 1.0
    slots = as_table(iota((SRC, count), 0) == rank.astype(jnp.int32))
    values = [lmn_ref[0:1, :], lmn_ref[1:2, :], lmn_ref[2:3, :], flux_ref[...]]
    pieces = [[], [], []]
    for value in values:
        for s, piece in enumerate(split3(value)):
            pieces[s].append(piece.astype(F32) * member_f)
    pieces = [jnp.concatenate(p, axis=0).astype(BF16) for p in pieces]
    along = chosen(pieces, slots)
    down = dot_nt(slots, pieces[2]) + dot_nt(slots, pieces[1]) + dot_nt(slots, pieces[0])
    sky_ref[...] = jnp.concatenate([along, along], axis=1)
    part_ref[...] = down
    xyz = [scale * moved[2 * DIRS + c : 2 * DIRS + c + 1, :] for c in range(3)]
    kept = station_at(iota((ROWS, STATIONS), 1)) != row_station((ROWS, STATIONS), 0, device)
    half = iota((1, LANES), 1) < SRC
    shift_real = jnp.where(half, 0.0, 0.25)
    shift_imag = jnp.where(half, 0.25, 0.5)
    for k in range(DIRS):
        column = [part_ref[:, c * DIRS + k : c * DIRS + k + 1] for c in range(3)]
        turns = wrapped(xyz[0] * column[0] + xyz[1] * column[1] + xyz[2] * column[2])
        wave = jnp.concatenate([cos_turns(turns), sin_turns(turns)], axis=0)
        wave_high, wave_low = split2(wave)
        row = [sky_ref[c * DIRS + k : c * DIRS + k + 1, :] for c in range(4)]
        turns = wrapped(own_xyz[0] * row[0] + own_xyz[1] * row[1] + own_xyz[2] * row[2])
        near = jnp.concatenate([cos_turns(wrapped(turns - shift_real)), cos_turns(wrapped(turns - shift_imag))], axis=0)
        near_high, near_low = split2(near * row[3])
        model = dot(near_high, wave_low) + dot(near_low, wave_high) + dot(near_high, wave_high)
        model_ref[k, 0:ROWS, :] = jnp.where(kept, model[0:ROWS, :], 0.0)
        model_ref[k, ROWS : 2 * ROWS, :] = jnp.where(kept, model[ROWS:, :], 0.0)
    for a in range(REPS):
        rows = slice(a * OWN, (a + 1) * OWN)
        pred_real, pred_imag, denom = predict(model_ref, gains_ref, own_ref[rows, :], a * OWN, None)
        pred_ref[rows, :] = pred_real
        pred_ref[ROWS + a * OWN : ROWS + (a + 1) * OWN, :] = pred_imag
        den_ref[rows, :] = denom


def gathered_gains(tiles_ref):
    turned = jnp.transpose(tiles_ref[...])
    return jnp.concatenate([turned[32 * a : 32 * a + 32, :] for a in range(4)], axis=1)


def channel_fit(near_ref, far_ref):
    channel = lax.axis_index("freq")
    total = None
    for d in range(CHANNELS // 2):
        other = (channel - 2 * d) & (CHANNELS - 1)
        for tiles_ref, source in ((near_ref, other), (far_ref, other ^ 1)):
            part = channel_weight(channel, source) * tiles_ref[d]
            total = part if total is None else total + part
    return unpacked(total)


def sums(model_ref, vis_ref, tiles_ref, own_ref, numer_ref, den_ref, along_ref, gains_ref):
    gains_ref[...] = gathered_gains(tiles_ref)
    for a in range(REPS):
        rows = slice(a * OWN, (a + 1) * OWN)
        numer, denom = row_sums(model_ref, vis_ref, gains_ref, own_ref[rows, :], a * OWN, along_ref)
        numer_ref[rows, :] = numer
        den_ref[rows, :] = denom


def first_kernel(tiles_ref, table_ref, model_ref, gains_ref, pred_ref, den_ref, own_ref, penalty_ref, vis_ref, state_ref, send_ref):
    turned = jnp.transpose(tiles_ref[...])
    pieces = split3(jnp.concatenate([turned[0 : 2 * ROWS, :], turned[2 * ROWS :, :]], axis=1))
    vis_ref[...] = chosen(pieces, table_ref[...])
    for a in range(REPS):
        rows = slice(a * OWN, (a + 1) * OWN)
        lower = slice(ROWS + a * OWN, ROWS + (a + 1) * OWN)
        resid_real = vis_ref[rows, :] - pred_ref[rows, :]
        resid_imag = vis_ref[lower, :] - pred_ref[lower, :]
        numer = correlate(resid_real, resid_imag, lambda k: products(model_ref, gains_ref, a * OWN, k))
        own = own_ref[rows, :]
        state_ref[rows, :] = updated(numer, den_ref[rows, :], own, own, penalty_ref[...])
    send_ref[...] = packed(state_ref[...])


def second_kernel(
    model_ref, vis_ref, tiles_ref, own_ref, anchor_ref, penalty_ref, state_ref, send_ref, along_ref, gains_ref, den_ref
):
    sums(model_ref, vis_ref, tiles_ref, own_ref, state_ref, den_ref, along_ref, gains_ref)
    state = updated(state_ref[...], den_ref[...], own_ref[...], anchor_ref[...], penalty_ref[...])
    state_ref[...] = state
    send_ref[...] = packed(state)


def anchor_kernel(numer_ref, den_ref, near_ref, far_ref, own_ref, penalty_ref, state_ref, anchor_ref, dual_ref, send_ref):
    own = own_ref[...]
    cons = channel_fit(near_ref, far_ref)
    dual = own - cons
    anchor = cons - dual
    state = updated(numer_ref[...], den_ref[...], own, anchor, penalty_ref[...])
    state_ref[...] = state
    send_ref[...] = packed(state)
    anchor_ref[...] = anchor
    dual_ref[...] = dual


def by_direction(state):
    filled = jnp.concatenate([state, jnp.zeros((LANES - OWN, LANES), F32)], axis=0)
    return jnp.transpose(filled)[0 : 2 * DIRS, 0:OWN]


def fourth_kernel(
    model_ref, vis_ref, tiles_ref, own_ref, anchor_ref, dual_ref, penalty_ref, state_ref, send_ref, along_ref, gains_ref
):
    start = pl.multiple_of(rep_of(lax.axis_index("stcol")) * OWN, OWN)
    rows = pl.ds(start, OWN)
    own = own_ref[rows, :]
    gains_ref[...] = gathered_gains(tiles_ref)
    numer, denom = row_sums(model_ref, vis_ref, gains_ref, own, start, along_ref)
    state = updated(numer, denom, own, anchor_ref[rows, :], penalty_ref[...])
    state_ref[...] = state
    send_ref[...] = packed(state + dual_ref[rows, :])


def last_kernel(tiles_ref, state_ref, out_ref, cons_ref):
    out_ref[...] = by_direction(state_ref[...])
    channel = lax.axis_index("freq")
    total = basis_product(channel, 0) * tiles_ref[0]
    for f in range(1, CHANNELS):
        total = total + basis_product(channel, f) * tiles_ref[f]
    cons_ref[...] = by_direction(unpacked(total))


def called(kernel, outs, scratch=(), name=None, in_specs=None):
    return pl.pallas_call(
        kernel,
        out_shape=[jax.ShapeDtypeStruct(*o) for o in outs],
        scratch_shapes=[pltpu.VMEM(*o) if isinstance(o, tuple) else o for o in scratch],
        compiler_params=pltpu.CompilerParams(vmem_limit_bytes=32 * 1024 * 1024),
        name=name,
        **({} if in_specs is None else {"in_specs": in_specs}),
    )


def held(x):
    return pltpu.with_memory_space_constraint(x, pltpu.HBM)


def to_all(tile, axis, count, groups=None):
    tiles = jnp.broadcast_to(tile, (count, *tile.shape))
    return lax.all_to_all(tiles, axis, 0, 0, tiled=True, axis_index_groups=groups)


def around(tile):
    return [tile] + [
        lax.ppermute(tile, "freq", [(i, (i + 2 * d) % CHANNELS) for i in range(CHANNELS)]) for d in range(1, CHANNELS // 2)
    ]


def both_cores(tiles):
    near = jnp.stack(tiles)
    return near, lax.ppermute(near, "freq", [(i, i ^ 1) for i in range(CHANNELS)])


def to_members(tile):
    members = [e ^ FRONT for e in range(MEMBERS)]
    groups = [[(e >> 2) * 8 + 4 * m + (e & 3) for e in members] for m in range(REPS)]
    return to_all(tile, "stcol", MEMBERS, groups).reshape(LANES, LANES)


def on_device(visibilities, positions, source_lmn, source_flux, cluster_map, station_order, penalty, offsets):
    hbm = pl.BlockSpec(memory_space=pltpu.HBM)
    vmem = pl.BlockSpec(memory_space=pltpu.VMEM)
    model_out = ((DIRS, 2 * ROWS, STATIONS), F32)
    along = ((DIRS, 2 * OWN, STATIONS), F32)
    vis_out = ((2 * ROWS, STATIONS), F32)
    state_out = ((ROWS, LANES), F32)
    send_out = ((ROWS // 4, LANES), F32)
    flat_out = ((2 * DIRS, OWN), F32)
    gains_out = ((2 * DIRS, STATIONS), F32)
    (tiles,) = called(
        turn_kernel,
        [((STATIONS // OWN, 8, LANES), F32)],
        [((2 * OWN, 1, STATIONS), F32), pltpu.SemaphoreType.DMA],
        "turn",
        [hbm],
    )(held(visibilities.reshape(2 * OWN, 1, STATIONS)))
    slots = [s ^ LEAD for s in range(STATIONS // OWN)]
    tiles = lax.all_to_all(tiles, "stcol", 0, 0, tiled=True, axis_index_groups=[slots]).reshape(STATIONS // 2, LANES)
    order = station_order.reshape(STATIONS // OWN, 2, 8)
    order = (order[::-1] if LEAD == 31 else order[jnp.array(slots)]).transpose(1, 0, 2).reshape(1, STATIONS)
    count = DIRS * SRC
    model, own, table, gains, pred, den, pen = called(
        model_kernel,
        [model_out, state_out, ((STATIONS, STATIONS), BF16), gains_out, vis_out, state_out, ((1, LANES), F32)],
        [
            gains_out, ((3, 1, STATIONS), F32), ((3, count), F32), ((1, count), F32), ((1, count), jnp.int32),
            pltpu.SMEM((1, DIRS), F32), ((4 * DIRS, 2 * SRC), F32), ((SRC, 4 * DIRS), F32),
            pltpu.SemaphoreType.DMA((6,)),
        ],
        "models",
        [hbm, hbm, hbm, hbm, hbm, vmem, hbm],
    )(
        held(offsets.reshape(2 * DIRS, STATIONS)), held(positions), held(source_lmn), held(source_flux.reshape(1, count)),
        held(cluster_map.reshape(1, count)), order, held(penalty.reshape(1, DIRS)),
    )
    vis, state, send = called(first_kernel, [vis_out, state_out, send_out], name="pass_one")(
        tiles, table, model, gains, pred, den, own, pen
    )
    got = to_members(send)
    state, send = called(second_kernel, [state_out, send_out], [along, gains_out, state_out], "pass_two")(
        model, vis, got, state, own, pen
    )
    near, far = both_cores(around(send))
    got = to_members(send)
    numer, den = called(sums, [state_out, state_out], [along, gains_out], "pass_three")(model, vis, got, state)
    state, anchor, dual, send = called(anchor_kernel, [state_out, state_out, state_out, send_out], name="update_three")(
        numer, den, near, far, state, pen
    )
    got = to_members(send)
    state, send = called(fourth_kernel, [((OWN, LANES), F32), ((4, LANES), F32)], [along, gains_out], "pass_four")(
        model, vis, got, state, anchor, dual, pen
    )
    out, cons = called(last_kernel, [flat_out, flat_out], name="consensus")(to_all(send, "freq", CHANNELS), state)
    shape = (2, 1, DIRS, OWN)
    return out.reshape(shape), cons.reshape(shape)


def solution(mesh):
    in_specs = (
        P(None, "freq", "stcol", None, None),
        P(),
        P(),
        P(),
        P(),
        P(),
        P(),
        P(None, "freq", None, None),
    )
    out_specs = (P(None, "freq", None, "stcol"), P(None, "freq", None, "stcol"))
    return jax.shard_map(
        on_device, mesh=mesh, in_specs=in_specs, out_specs=out_specs, check_vma=False
    )
```

```python
import math

import jax
import jax.numpy as jnp
import numpy as np
from jax import lax
from jax.experimental import pallas as pl
from jax.experimental.pallas import tpu as pltpu
from jax.sharding import PartitionSpec as P

STATIONS = 512
DIRS = 16
SRC = 64
CHANNELS = 8
OWN = 16
REPS = 2
ROWS = REPS * OWN
MEMBERS = STATIONS // ROWS
LANES = 128
FRONT = 10
LEAD = 31
HEAD = 4
F32 = jnp.float32
BF16 = jnp.bfloat16

COS_TERMS = None
SIN_TERMS = None


def fit_terms():
    nodes = np.cos(np.pi * (np.arange(400) + 0.5) / 400)
    u = 0.125 * (nodes + 1.0)
    r = np.sqrt(u)
    cheb = np.polynomial.chebyshev
    poly = np.polynomial.polynomial

    def terms(values, degree):
        series = cheb.cheb2poly(cheb.chebfit(nodes, values, degree))
        out = np.zeros(1)
        for c in series[::-1]:
            out = poly.polyadd(poly.polymul(out, [-1.0, 8.0]), [c])
        return [float(np.float32(c)) for c in out[: degree + 1]]

    return terms(np.cos(2 * np.pi * r), 7), terms(np.sin(2 * np.pi * r) / r, 6)


COS_TERMS, SIN_TERMS = fit_terms()


def basis_table():
    centre = (np.arange(CHANNELS) - 0.5 * (CHANNELS - 1)) / CHANNELS
    columns = [np.ones_like(centre), centre, centre * centre]
    finished = []
    for column in columns:
        for before in finished:
            column = column - np.sum(column * before) * before
        finished.append(column / np.sqrt(np.sum(column * column)))
    return np.stack(finished, axis=1)


BASIS = basis_table()


def basis_row(channel):
    centre = (np.arange(CHANNELS) - 0.5 * (CHANNELS - 1)) / CHANNELS
    square = centre * centre
    flat = BASIS[:, 0]
    lift = float(np.sum(square * flat))
    norm1 = float(np.sqrt(np.sum(centre * centre)))
    norm2 = float(np.sqrt(np.sum((square - lift * flat) ** 2)))
    x = (channel.astype(F32) - 0.5 * (CHANNELS - 1)) * (1.0 / CHANNELS)
    return (float(flat[0]), x * (1.0 / norm1), (x * x - lift * float(flat[0])) * (1.0 / norm2))


def channel_weight(channel, source):
    return sum(a * b for a, b in zip(basis_row(channel), basis_row(source)))


def basis_product(channel, source):
    return sum(a * float(b) for a, b in zip(basis_row(channel), BASIS[source]))


def horner(u, terms):
    out = jnp.full_like(u, terms[-1])
    for c in terms[-2::-1]:
        out = out * u + c
    return out


def wrapped(turns):
    return turns - jnp.round(turns)


def cos_turns(r):
    return horner(r * r, COS_TERMS)


def sin_turns(r):
    return r * horner(r * r, SIN_TERMS)


def split2(x):
    high = x.astype(BF16)
    return high, (x - high.astype(F32)).astype(BF16)


def split3(x):
    high = x.astype(BF16)
    rest = x - high.astype(F32)
    mid = rest.astype(BF16)
    return high, mid, (rest - mid.astype(F32)).astype(BF16)


def dot(a, b):
    return lax.dot_general(a, b, (((1,), (0,)), ((), ())), preferred_element_type=F32)


def dot_nt(a, b):
    return lax.dot_general(a, b, (((1,), (1,)), ((), ())), preferred_element_type=F32)


def chosen(pieces, table):
    return dot_nt(pieces[2], table) + dot_nt(pieces[1], table) + dot_nt(pieces[0], table)


def iota(shape, dim):
    return lax.broadcasted_iota(jnp.int32, shape, dim)


def as_table(cond):
    return jnp.where(cond, jnp.ones(cond.shape, F32), jnp.zeros(cond.shape, F32)).astype(BF16)


def station_at(place):
    member = ((place >> 3) & 15) ^ FRONT
    return ((member >> 2) << 7) + ((place >> 8) << 6) + ((member & 3) << 4) + (((place >> 7) & 1) << 3) + (place & 7)


def row_station(shape, dim, device):
    row = iota(shape, dim)
    return ((row >> 4) << 6) + (row & 15) + ((device >> 3) << 7) + ((device & 3) << 4)


def rep_of(device):
    return (device & 7) >> 2


def packed(state):
    n = state.shape[0] // 4
    out = state[0:n, :]
    for a in range(1, 4):
        out = out + pltpu.roll(state, 32 * a, 1)[n * a : n * a + n, :]
    return out


def unpacked(tile):
    rows = [tile] + [pltpu.roll(tile, LANES - 32 * a, 1) for a in range(1, 4)]
    both = jnp.concatenate(rows, axis=0)
    return jnp.where(iota(both.shape, 1) < 2 * DIRS, both, 0.0)


def turn_kernel(vis_hbm, tiles_ref, vis_ref, sem):
    copy = pltpu.make_async_copy(vis_hbm, vis_ref, sem)
    copy.start()
    copy.wait()
    lane = iota((8, LANES), 1)
    for x in range(4):
        parts = [vis_ref[r * 8 : (r + 1) * 8, 0, x * LANES : (x + 1) * LANES] for r in range(4)]
        for b in range(4):
            tile = jnp.zeros((8, LANES), F32)
            for half in range(2):
                for r in range(2):
                    for a in range(REPS):
                        to = half * 64 + r * ROWS + a * OWN
                        moved = pltpu.roll(parts[2 * r + half], (to - (64 * a + 16 * b)) % LANES, 1)
                        tile = jnp.where((lane >> 4) == (to >> 4), moved, tile)
            for a in range(REPS):
                tiles_ref[(x * 8 + 4 * a + b) ^ LEAD] = tile


def products(model_ref, gains_ref, start, k, lanes=slice(None)):
    half = model_ref.shape[1] // 2
    model_real = model_ref[k, pl.ds(start, OWN), lanes]
    model_imag = model_ref[k, pl.ds(start + half, OWN), lanes]
    col_real = gains_ref[k : k + 1, lanes]
    col_imag = gains_ref[DIRS + k : DIRS + k + 1, lanes]
    return model_real * col_real + model_imag * col_imag, model_imag * col_real - model_real * col_imag


def predict(model_ref, gains_ref, own, start):
    pred_real = jnp.zeros((OWN, STATIONS), F32)
    pred_imag = jnp.zeros((OWN, STATIONS), F32)
    lane = iota((OWN, LANES), 1)
    denom = jnp.zeros((OWN, LANES), F32)
    for k in range(DIRS):
        along_real, along_imag = products(model_ref, gains_ref, start, k)
        row_real = own[:, k : k + 1]
        row_imag = own[:, DIRS + k : DIRS + k + 1]
        pred_real = pred_real + (row_real * along_real - row_imag * along_imag)
        pred_imag = pred_imag + (row_real * along_imag + row_imag * along_real)
        den = jnp.sum(along_real * along_real + along_imag * along_imag, axis=1, keepdims=True)
        denom = jnp.where((lane == k) | (lane == DIRS + k), den, denom)
    return pred_real, pred_imag, denom


def lane_sums(part_ref):
    shape = part_ref.shape
    high, low = split2(part_ref[...].reshape(-1, LANES))
    ones = jnp.ones((LANES, LANES), BF16)
    return (dot(low, ones) + dot(high, ones)).reshape(shape)


def by_lane(real, imag, rows):
    lane = iota((rows, LANES), 1)
    out = jnp.zeros((rows, LANES), F32)
    for k in range(DIRS):
        out = jnp.where(lane == k, real(k), jnp.where(lane == DIRS + k, imag(k), out))
    return out


def pieces_of(t):
    return slice(t * LANES, (t + 1) * LANES)


def row_sums(model_ref, vis_ref, turned, own, start, along_ref, part_ref):
    n = own.shape[0]
    real_rows, imag_rows = pl.ds(start, n), pl.ds(start + ROWS, n)
    pred_real = [jnp.zeros((n, LANES), F32)] * 4
    pred_imag = [jnp.zeros((n, LANES), F32)] * 4
    for k in range(DIRS):
        row_real = jnp.broadcast_to(own[:, k : k + 1], (n, LANES))
        row_imag = jnp.broadcast_to(own[:, DIRS + k : DIRS + k + 1], (n, LANES))
        squares = None
        for t in range(4):
            col_real = turned[32 * t + k : 32 * t + k + 1, :]
            col_imag = turned[32 * t + DIRS + k : 32 * t + DIRS + k + 1, :]
            model_real = model_ref[k, real_rows, pieces_of(t)]
            model_imag = model_ref[k, imag_rows, pieces_of(t)]
            along_real = model_real * col_real + model_imag * col_imag
            along_imag = model_imag * col_real - model_real * col_imag
            along_ref[k, 0:n, pieces_of(t)] = along_real
            along_ref[k, n : 2 * n, pieces_of(t)] = along_imag
            pred_real[t] = pred_real[t] + (row_real * along_real - row_imag * along_imag)
            pred_imag[t] = pred_imag[t] + (row_real * along_imag + row_imag * along_real)
            square = along_real * along_real + along_imag * along_imag
            squares = square if squares is None else squares + square
        part_ref[2, k] = squares
    resid_real = [vis_ref[real_rows, pieces_of(t)] - pred_real[t] for t in range(4)]
    resid_imag = [vis_ref[imag_rows, pieces_of(t)] - pred_imag[t] for t in range(4)]
    correlate(resid_real, resid_imag, lambda k, t: (along_ref[k, 0:n, pieces_of(t)], along_ref[k, n : 2 * n, pieces_of(t)]), part_ref)
    sums = lane_sums(part_ref)
    return by_lane(lambda k: sums[0, k], lambda k: sums[1, k], n), by_lane(lambda k: sums[2, k], lambda k: sums[2, k], n)


def correlate(resid_real, resid_imag, along, part_ref):
    for k in range(DIRS):
        real = imag = None
        for t in range(4):
            along_real, along_imag = along(k, t)
            u = resid_real[t] * along_real + resid_imag[t] * along_imag
            v = resid_imag[t] * along_real - resid_real[t] * along_imag
            real = u if real is None else real + u
            imag = v if imag is None else imag + v
        part_ref[0, k] = real
        part_ref[1, k] = imag


def updated(numer, denom, own, anchor, penalty):
    fresh = (numer + own * denom + penalty * anchor) / (denom + penalty)
    return jnp.where(iota(own.shape, 1) < 2 * DIRS, 0.5 * (own + fresh), 0.0)


def model_kernel(
    offs_hbm, place_hbm, lmn_hbm, flux_hbm, map_hbm, order_ref, penalty_hbm,
    model_ref, own_ref, table_ref, gains_ref, pred_ref, den_ref, weight_ref,
    offs_ref, xyz_ref, lmn_ref, flux_ref, map_ref, penalty_ref, sky_ref, part_ref, sems,
):
    pairs = [
        (map_hbm, map_ref), (lmn_hbm, lmn_ref), (flux_hbm, flux_ref),
        (offs_hbm, offs_ref), (place_hbm, xyz_ref), (penalty_hbm, penalty_ref),
    ]
    copies = [pltpu.make_async_copy(a, b, sems.at[n]) for n, (a, b) in enumerate(pairs)]
    for copy in copies:
        copy.start()
    device = lax.axis_index("stcol")
    scale = 1.0 + 0.5 * lax.axis_index("freq").astype(F32) / CHANNELS
    for copy in copies:
        copy.wait()
    lane = iota((1, LANES), 1)
    weight = jnp.ones((1, LANES), F32)
    for k in range(DIRS):
        weight = jnp.where((lane == k) | (lane == DIRS + k), penalty_ref[0, k], weight)
    weight_ref[...] = weight
    offs = offs_ref[...]
    rows = [1.0 + offs[0:DIRS, :], offs[DIRS : 2 * DIRS, :]] + [xyz_ref[c] for c in range(3)]
    pieces = split3(jnp.concatenate(rows + [jnp.zeros((5, STATIONS), F32)], axis=0))
    place = station_at(iota((STATIONS, STATIONS), 0))
    moved = chosen(pieces, as_table(place == iota((STATIONS, STATIONS), 1)))
    gains_ref[...] = moved[0 : 2 * DIRS, :]
    table_ref[...] = as_table(place == order_ref[...])
    mine = as_table(iota((ROWS, STATIONS), 1) == row_station((ROWS, STATIONS), 0, device))
    own = sum(dot_nt(mine, piece) for piece in pieces[::-1])
    own = jnp.concatenate([own, jnp.zeros((ROWS, LANES - own.shape[1]), F32)], axis=1)
    own_xyz = [scale * own[:, 2 * DIRS + c : 2 * DIRS + c + 1] for c in range(3)]
    own_ref[...] = jnp.where(iota(own.shape, 1) < 2 * DIRS, own, 0.0)
    count = DIRS * SRC
    member = map_ref[...] == iota((DIRS, count), 0)
    member_f = jnp.where(member, 1.0, 0.0)
    blocks = count // LANES
    stacked = jnp.concatenate([member_f[:, b * LANES : (b + 1) * LANES] for b in range(blocks)], axis=0)
    ahead = as_table(iota((LANES, LANES), 0) <= iota((LANES, LANES), 1))
    running = dot(stacked.astype(BF16), ahead)
    carried = jnp.zeros((DIRS, 1), F32)
    ranks = []
    for b in range(blocks):
        here = running[b * DIRS : (b + 1) * DIRS, :] + carried
        ranks.append(jnp.sum(here * member_f[:, b * LANES : (b + 1) * LANES], axis=0, keepdims=True))
        carried = here[:, LANES - 1 : LANES]
    rank = jnp.concatenate(ranks, axis=1) - 1.0
    slots = as_table(iota((SRC, count), 0) == rank.astype(jnp.int32))
    values = [lmn_ref[0:1, :], lmn_ref[1:2, :], lmn_ref[2:3, :], flux_ref[...]]
    pieces = [[], [], []]
    for value in values:
        for s, piece in enumerate(split3(value)):
            pieces[s].append(piece.astype(F32) * member_f)
    pieces = [jnp.concatenate(p, axis=0).astype(BF16) for p in pieces]
    along = chosen(pieces, slots)
    down = dot_nt(slots, pieces[2]) + dot_nt(slots, pieces[1]) + dot_nt(slots, pieces[0])
    sky_ref[...] = jnp.concatenate([along, along], axis=1)
    part_ref[...] = down
    xyz = [scale * moved[2 * DIRS + c : 2 * DIRS + c + 1, :] for c in range(3)]
    kept = station_at(iota((ROWS, STATIONS), 1)) != row_station((ROWS, STATIONS), 0, device)
    half = iota((1, LANES), 1) < SRC
    shift_real = jnp.where(half, 0.0, 0.25)
    shift_imag = jnp.where(half, 0.25, 0.5)
    for k in range(DIRS):
        column = [part_ref[:, c * DIRS + k : c * DIRS + k + 1] for c in range(3)]
        turns = wrapped(xyz[0] * column[0] + xyz[1] * column[1] + xyz[2] * column[2])
        wave = jnp.concatenate([cos_turns(turns), sin_turns(turns)], axis=0)
        wave_high, wave_low = split2(wave)
        row = [sky_ref[c * DIRS + k : c * DIRS + k + 1, :] for c in range(4)]
        turns = wrapped(own_xyz[0] * row[0] + own_xyz[1] * row[1] + own_xyz[2] * row[2])
        near = jnp.concatenate([cos_turns(wrapped(turns - shift_real)), cos_turns(wrapped(turns - shift_imag))], axis=0)
        near_high, near_low = split2(near * row[3])
        model = dot(near_high, wave_low) + dot(near_low, wave_high) + dot(near_high, wave_high)
        model_ref[k, 0:ROWS, :] = jnp.where(kept, model[0:ROWS, :], 0.0)
        model_ref[k, ROWS : 2 * ROWS, :] = jnp.where(kept, model[ROWS:, :], 0.0)
    for a in range(REPS):
        rows = slice(a * OWN, (a + 1) * OWN)
        pred_real, pred_imag, denom = predict(model_ref, gains_ref, own_ref[rows, :], a * OWN)
        pred_ref[rows, :] = pred_real
        pred_ref[ROWS + a * OWN : ROWS + (a + 1) * OWN, :] = pred_imag
        den_ref[rows, :] = denom


def channel_fit(near_ref, far_ref):
    channel = lax.axis_index("freq")
    total = None
    for d in range(CHANNELS // 2):
        other = (channel - 2 * d) & (CHANNELS - 1)
        for tiles_ref, source in ((near_ref, other), (far_ref, other ^ 1)):
            part = channel_weight(channel, source) * tiles_ref[d]
            total = part if total is None else total + part
    return unpacked(total)


def sums(model_ref, vis_ref, tiles_ref, own_ref, numer_ref, den_ref, along_ref, part_ref):
    turned = jnp.transpose(tiles_ref[...])
    numer_ref[...], den_ref[...] = row_sums(model_ref, vis_ref, turned, own_ref[...], 0, along_ref, part_ref)


def first_kernel(
    tiles_ref, table_ref, model_ref, gains_ref, pred_ref, den_ref, own_ref, penalty_ref, vis_ref, state_ref, send_ref, part_ref
):
    turned = jnp.transpose(tiles_ref[...])
    pieces = split3(jnp.concatenate([turned[0 : 2 * ROWS, :], turned[2 * ROWS :, :]], axis=1))
    vis_ref[...] = chosen(pieces, table_ref[...])
    for a in range(REPS):
        rows = slice(a * OWN, (a + 1) * OWN)
        lower = slice(ROWS + a * OWN, ROWS + (a + 1) * OWN)
        resid_real = [vis_ref[rows, pieces_of(t)] - pred_ref[rows, pieces_of(t)] for t in range(4)]
        resid_imag = [vis_ref[lower, pieces_of(t)] - pred_ref[lower, pieces_of(t)] for t in range(4)]
        correlate(resid_real, resid_imag, lambda k, t: products(model_ref, gains_ref, a * OWN, k, pieces_of(t)), part_ref.at[:, :, rows])
    total = lane_sums(part_ref)
    numer = by_lane(lambda k: total[0, k], lambda k: total[1, k], ROWS)
    own = own_ref[...]
    state = updated(numer, den_ref[...], own, own, penalty_ref[...])
    state_ref[...] = state
    send_ref[...] = packed(state)


def second_kernel(
    model_ref, vis_ref, tiles_ref, own_ref, anchor_ref, penalty_ref, state_ref, send_ref, along_ref, part_ref
):
    turned = jnp.transpose(tiles_ref[...])
    own = own_ref[...]
    numer, denom = row_sums(model_ref, vis_ref, turned, own, 0, along_ref, part_ref)
    state = updated(numer, denom, own, anchor_ref[...], penalty_ref[...])
    state_ref[...] = state
    send_ref[...] = packed(state)


def anchor_kernel(numer_ref, den_ref, near_ref, far_ref, own_ref, penalty_ref, state_ref, anchor_ref, dual_ref, send_ref):
    own = own_ref[...]
    cons = channel_fit(near_ref, far_ref)
    dual = own - cons
    anchor = cons - dual
    state = updated(numer_ref[...], den_ref[...], own, anchor, penalty_ref[...])
    state_ref[...] = state
    send_ref[...] = packed(state)
    anchor_ref[...] = anchor
    dual_ref[...] = dual


def by_direction(state):
    filled = jnp.concatenate([state, jnp.zeros((LANES - OWN, LANES), F32)], axis=0)
    return jnp.transpose(filled)[0 : 2 * DIRS, 0:OWN]


def fourth_kernel(
    model_ref, vis_ref, tiles_ref, own_ref, anchor_ref, dual_ref, penalty_ref, state_ref, send_ref, along_ref, part_ref
):
    start = pl.multiple_of(rep_of(lax.axis_index("stcol")) * OWN, OWN)
    rows = pl.ds(start, OWN)
    own = own_ref[rows, :]
    turned = jnp.transpose(tiles_ref[...])
    numer, denom = row_sums(model_ref, vis_ref, turned, own, start, along_ref, part_ref)
    state = updated(numer, denom, own, anchor_ref[rows, :], penalty_ref[...])
    state_ref[...] = state
    send_ref[...] = packed(state + dual_ref[rows, :])


def last_kernel(tiles_ref, state_ref, out_ref, cons_ref):
    out_ref[...] = by_direction(state_ref[...])
    channel = lax.axis_index("freq")
    total = basis_product(channel, HEAD) * tiles_ref[0]
    for f in range(1, CHANNELS):
        total = total + basis_product(channel, f ^ HEAD) * tiles_ref[f]
    cons_ref[...] = by_direction(unpacked(total))


def called(kernel, outs, scratch=(), name=None, in_specs=None):
    return pl.pallas_call(
        kernel,
        out_shape=[jax.ShapeDtypeStruct(*o) for o in outs],
        scratch_shapes=[pltpu.VMEM(*o) if isinstance(o, tuple) else o for o in scratch],
        compiler_params=pltpu.CompilerParams(vmem_limit_bytes=32 * 1024 * 1024),
        name=name,
        **({} if in_specs is None else {"in_specs": in_specs}),
    )


def held(x):
    return pltpu.with_memory_space_constraint(x, pltpu.HBM)


def to_all(tile, axis, count, groups=None):
    tiles = jnp.broadcast_to(tile, (count, *tile.shape))
    return lax.all_to_all(tiles, axis, 0, 0, tiled=True, axis_index_groups=groups)


def around(tile):
    return [tile] + [
        lax.ppermute(tile, "freq", [(i, (i + 2 * d) % CHANNELS) for i in range(CHANNELS)]) for d in range(1, CHANNELS // 2)
    ]


def both_cores(tiles):
    near = jnp.stack(tiles)
    return near, lax.ppermute(near, "freq", [(i, i ^ 1) for i in range(CHANNELS)])


def to_members(tile):
    members = [e ^ FRONT for e in range(MEMBERS)]
    groups = [[(e >> 2) * 8 + 4 * m + (e & 3) for e in members] for m in range(REPS)]
    return to_all(tile, "stcol", MEMBERS, groups).reshape(LANES, LANES)


def on_device(visibilities, positions, source_lmn, source_flux, cluster_map, station_order, penalty, offsets):
    hbm = pl.BlockSpec(memory_space=pltpu.HBM)
    vmem = pl.BlockSpec(memory_space=pltpu.VMEM)
    model_out = ((DIRS, 2 * ROWS, STATIONS), F32)
    along = ((DIRS, 2 * OWN, STATIONS), F32)
    part = ((3, DIRS, OWN, LANES), F32)
    parts = ((3, DIRS, ROWS, LANES), F32)
    vis_out = ((2 * ROWS, STATIONS), F32)
    state_out = ((ROWS, LANES), F32)
    send_out = ((ROWS // 4, LANES), F32)
    flat_out = ((2 * DIRS, OWN), F32)
    gains_out = ((2 * DIRS, STATIONS), F32)
    (tiles,) = called(
        turn_kernel,
        [((STATIONS // OWN, 8, LANES), F32)],
        [((2 * OWN, 1, STATIONS), F32), pltpu.SemaphoreType.DMA],
        "turn",
        [hbm],
    )(held(visibilities.reshape(2 * OWN, 1, STATIONS)))
    slots = [s ^ LEAD for s in range(STATIONS // OWN)]
    tiles = lax.all_to_all(tiles, "stcol", 0, 0, tiled=True, axis_index_groups=[slots]).reshape(STATIONS // 2, LANES)
    order = station_order.reshape(STATIONS // OWN, 2, 8)
    order = (order[::-1] if LEAD == 31 else order[jnp.array(slots)]).transpose(1, 0, 2).reshape(1, STATIONS)
    count = DIRS * SRC
    model, own, table, gains, pred, den, pen = called(
        model_kernel,
        [model_out, state_out, ((STATIONS, STATIONS), BF16), gains_out, vis_out, state_out, ((1, LANES), F32)],
        [
            gains_out, ((3, 1, STATIONS), F32), ((3, count), F32), ((1, count), F32), ((1, count), jnp.int32),
            pltpu.SMEM((1, DIRS), F32), ((4 * DIRS, 2 * SRC), F32), ((SRC, 4 * DIRS), F32),
            pltpu.SemaphoreType.DMA((6,)),
        ],
        "models",
        [hbm, hbm, hbm, hbm, hbm, vmem, hbm],
    )(
        held(offsets.reshape(2 * DIRS, STATIONS)), held(positions), held(source_lmn), held(source_flux.reshape(1, count)),
        held(cluster_map.reshape(1, count)), order, held(penalty.reshape(1, DIRS)),
    )
    vis, state, send = called(first_kernel, [vis_out, state_out, send_out], [((2, DIRS, ROWS, LANES), F32)], "pass_one")(
        tiles, table, model, gains, pred, den, own, pen
    )
    got = to_members(send)
    state, send = called(second_kernel, [state_out, send_out], [model_out, parts], "pass_two")(
        model, vis, got, state, own, pen
    )
    tiles = around(send)
    got = to_members(send)
    numer, den = called(sums, [state_out, state_out], [model_out, parts], "pass_three")(model, vis, got, state)
    near, far = both_cores(lax.optimization_barrier((*tiles, got))[:-1])
    state, anchor, dual, send = called(anchor_kernel, [state_out, state_out, state_out, send_out], name="update_three")(
        numer, den, near, far, state, pen
    )
    got = to_members(send)
    state, send = called(fourth_kernel, [((OWN, LANES), F32), ((4, LANES), F32)], [along, part], "pass_four")(
        model, vis, got, state, anchor, dual, pen
    )
    out, cons = called(last_kernel, [flat_out, flat_out], name="consensus")(to_all(send, "freq", CHANNELS, [[f ^ HEAD for f in range(CHANNELS)]]), state)
    shape = (2, 1, DIRS, OWN)
    return out.reshape(shape), cons.reshape(shape)


def solution(mesh):
    in_specs = (
        P(None, "freq", "stcol", None, None),
        P(),
        P(),
        P(),
        P(),
        P(),
        P(),
        P(None, "freq", None, None),
    )
    out_specs = (P(None, "freq", None, "stcol"), P(None, "freq", None, "stcol"))
    return jax.shard_map(
        on_device, mesh=mesh, in_specs=in_specs, out_specs=out_specs, check_vma=False
    )
```

```python
import math

import jax
import jax.numpy as jnp
import numpy as np
from jax import lax
from jax.experimental import pallas as pl
from jax.experimental.pallas import tpu as pltpu
from jax.sharding import PartitionSpec as P

STATIONS = 512
DIRS = 16
SRC = 64
CHANNELS = 8
OWN = 16
REPS = 2
ROWS = REPS * OWN
MEMBERS = STATIONS // ROWS
LANES = 128
FRONT = 10
LEAD = 31
HEAD = 4
F32 = jnp.float32
BF16 = jnp.bfloat16

COS_TERMS = None
SIN_TERMS = None


def fit_terms():
    nodes = np.cos(np.pi * (np.arange(400) + 0.5) / 400)
    u = 0.125 * (nodes + 1.0)
    r = np.sqrt(u)
    cheb = np.polynomial.chebyshev
    poly = np.polynomial.polynomial

    def terms(values, degree):
        series = cheb.cheb2poly(cheb.chebfit(nodes, values, degree))
        out = np.zeros(1)
        for c in series[::-1]:
            out = poly.polyadd(poly.polymul(out, [-1.0, 8.0]), [c])
        return [float(np.float32(c)) for c in out[: degree + 1]]

    return terms(np.cos(2 * np.pi * r), 6), terms(np.sin(2 * np.pi * r) / r, 6)


COS_TERMS, SIN_TERMS = fit_terms()


def basis_table():
    centre = (np.arange(CHANNELS) - 0.5 * (CHANNELS - 1)) / CHANNELS
    columns = [np.ones_like(centre), centre, centre * centre]
    finished = []
    for column in columns:
        for before in finished:
            column = column - np.sum(column * before) * before
        finished.append(column / np.sqrt(np.sum(column * column)))
    return np.stack(finished, axis=1)


BASIS = basis_table()


def basis_row(channel):
    centre = (np.arange(CHANNELS) - 0.5 * (CHANNELS - 1)) / CHANNELS
    square = centre * centre
    flat = BASIS[:, 0]
    lift = float(np.sum(square * flat))
    norm1 = float(np.sqrt(np.sum(centre * centre)))
    norm2 = float(np.sqrt(np.sum((square - lift * flat) ** 2)))
    x = (channel.astype(F32) - 0.5 * (CHANNELS - 1)) * (1.0 / CHANNELS)
    return (float(flat[0]), x * (1.0 / norm1), (x * x - lift * float(flat[0])) * (1.0 / norm2))


def channel_weight(channel, source):
    return sum(a * b for a, b in zip(basis_row(channel), basis_row(source)))


def basis_product(channel, source):
    return sum(a * float(b) for a, b in zip(basis_row(channel), BASIS[source]))


def horner(u, terms):
    out = jnp.full_like(u, terms[-1])
    for c in terms[-2::-1]:
        out = out * u + c
    return out


def wrapped(turns):
    return turns - ((turns + 12582912.0) - 12582912.0)


def cos_turns(r):
    return horner(r * r, COS_TERMS)


def sin_turns(r):
    return r * horner(r * r, SIN_TERMS)


def split2(x):
    high = x.astype(BF16)
    return high, (x - high.astype(F32)).astype(BF16)


def split3(x):
    high = x.astype(BF16)
    rest = x - high.astype(F32)
    mid = rest.astype(BF16)
    return high, mid, (rest - mid.astype(F32)).astype(BF16)


def dot(a, b):
    return lax.dot_general(a, b, (((1,), (0,)), ((), ())), preferred_element_type=F32)


def dot_nt(a, b):
    return lax.dot_general(a, b, (((1,), (1,)), ((), ())), preferred_element_type=F32)


def chosen(pieces, table):
    return dot_nt(pieces[2], table) + dot_nt(pieces[1], table) + dot_nt(pieces[0], table)


def iota(shape, dim):
    return lax.broadcasted_iota(jnp.int32, shape, dim)


def as_table(cond):
    return jnp.where(cond, jnp.ones(cond.shape, F32), jnp.zeros(cond.shape, F32)).astype(BF16)


def station_at(place):
    member = ((place >> 3) & 15) ^ FRONT
    return ((member >> 2) << 7) + ((place >> 8) << 6) + ((member & 3) << 4) + (((place >> 7) & 1) << 3) + (place & 7)


def row_station(shape, dim, device):
    row = iota(shape, dim)
    return ((row >> 4) << 6) + (row & 15) + ((device >> 3) << 7) + ((device & 3) << 4)


def rep_of(device):
    return (device & 7) >> 2


def packed(state):
    n = state.shape[0] // 4
    out = state[0:n, :]
    for a in range(1, 4):
        out = out + pltpu.roll(state, 32 * a, 1)[n * a : n * a + n, :]
    return out


def unpacked(tile):
    rows = [tile] + [pltpu.roll(tile, LANES - 32 * a, 1) for a in range(1, 4)]
    both = jnp.concatenate(rows, axis=0)
    return jnp.where(iota(both.shape, 1) < 2 * DIRS, both, 0.0)


def turn_kernel(vis_hbm, tiles_ref, vis_ref, sem):
    copy = pltpu.make_async_copy(vis_hbm, vis_ref, sem)
    copy.start()
    copy.wait()
    lane = iota((8, LANES), 1)
    for x in range(4):
        parts = [vis_ref[r * 8 : (r + 1) * 8, 0, x * LANES : (x + 1) * LANES] for r in range(4)]
        for b in range(4):
            tile = jnp.zeros((8, LANES), F32)
            for half in range(2):
                for r in range(2):
                    for a in range(REPS):
                        to = half * 64 + r * ROWS + a * OWN
                        moved = pltpu.roll(parts[2 * r + half], (to - (64 * a + 16 * b)) % LANES, 1)
                        tile = jnp.where((lane >> 4) == (to >> 4), moved, tile)
            for a in range(REPS):
                tiles_ref[(x * 8 + 4 * a + b) ^ LEAD] = tile


def products(model_ref, gains_ref, start, k, lanes=slice(None)):
    half = model_ref.shape[1] // 2
    model_real = model_ref[k, pl.ds(start, OWN), lanes]
    model_imag = model_ref[k, pl.ds(start + half, OWN), lanes]
    col_real = gains_ref[k : k + 1, lanes]
    col_imag = gains_ref[DIRS + k : DIRS + k + 1, lanes]
    return model_real * col_real + model_imag * col_imag, model_imag * col_real - model_real * col_imag


def predict(model_ref, gains_ref, own, start):
    pred_real = jnp.zeros((OWN, STATIONS), F32)
    pred_imag = jnp.zeros((OWN, STATIONS), F32)
    lane = iota((OWN, LANES), 1)
    denom = jnp.zeros((OWN, LANES), F32)
    for k in range(DIRS):
        along_real, along_imag = products(model_ref, gains_ref, start, k)
        row_real = own[:, k : k + 1]
        row_imag = own[:, DIRS + k : DIRS + k + 1]
        pred_real = pred_real + (row_real * along_real - row_imag * along_imag)
        pred_imag = pred_imag + (row_real * along_imag + row_imag * along_real)
        den = jnp.sum(along_real * along_real + along_imag * along_imag, axis=1, keepdims=True)
        denom = jnp.where((lane == k) | (lane == DIRS + k), den, denom)
    return pred_real, pred_imag, denom


def lane_sums(part_ref):
    shape = part_ref.shape
    high, low = split2(part_ref[...].reshape(-1, LANES))
    ones = jnp.ones((LANES, LANES), BF16)
    return (dot(low, ones) + dot(high, ones)).reshape(shape)


def by_lane(real, imag, rows):
    lane = iota((rows, LANES), 1)
    out = jnp.zeros((rows, LANES), F32)
    for k in range(DIRS):
        out = jnp.where(lane == k, real(k), jnp.where(lane == DIRS + k, imag(k), out))
    return out


def pieces_of(t):
    return slice(t * LANES, (t + 1) * LANES)


def row_sums(model_ref, vis_ref, turned, own, start, along_ref, part_ref):
    n = own.shape[0]
    real_rows, imag_rows = pl.ds(start, n), pl.ds(start + ROWS, n)
    pred_real = [jnp.zeros((n, LANES), F32)] * 4
    pred_imag = [jnp.zeros((n, LANES), F32)] * 4
    for k in range(DIRS):
        row_real = jnp.broadcast_to(own[:, k : k + 1], (n, LANES))
        row_imag = jnp.broadcast_to(own[:, DIRS + k : DIRS + k + 1], (n, LANES))
        squares = None
        for t in range(4):
            col_real = turned[32 * t + k : 32 * t + k + 1, :]
            col_imag = turned[32 * t + DIRS + k : 32 * t + DIRS + k + 1, :]
            model_real = model_ref[k, real_rows, pieces_of(t)]
            model_imag = model_ref[k, imag_rows, pieces_of(t)]
            along_real = model_real * col_real + model_imag * col_imag
            along_imag = model_imag * col_real - model_real * col_imag
            along_ref[k, 0:n, pieces_of(t)] = along_real
            along_ref[k, n : 2 * n, pieces_of(t)] = along_imag
            pred_real[t] = pred_real[t] + (row_real * along_real - row_imag * along_imag)
            pred_imag[t] = pred_imag[t] + (row_real * along_imag + row_imag * along_real)
            square = along_real * along_real + along_imag * along_imag
            squares = square if squares is None else squares + square
        part_ref[2, k] = squares
    resid_real = [vis_ref[real_rows, pieces_of(t)] - pred_real[t] for t in range(4)]
    resid_imag = [vis_ref[imag_rows, pieces_of(t)] - pred_imag[t] for t in range(4)]
    correlate(resid_real, resid_imag, lambda k, t: (along_ref[k, 0:n, pieces_of(t)], along_ref[k, n : 2 * n, pieces_of(t)]), part_ref)
    sums = lane_sums(part_ref)
    return by_lane(lambda k: sums[0, k], lambda k: sums[1, k], n), by_lane(lambda k: sums[2, k], lambda k: sums[2, k], n)


def correlate(resid_real, resid_imag, along, part_ref):
    for k in range(DIRS):
        real = imag = None
        for t in range(4):
            along_real, along_imag = along(k, t)
            u = resid_real[t] * along_real + resid_imag[t] * along_imag
            v = resid_imag[t] * along_real - resid_real[t] * along_imag
            real = u if real is None else real + u
            imag = v if imag is None else imag + v
        part_ref[0, k] = real
        part_ref[1, k] = imag


def updated(numer, denom, own, anchor, penalty):
    fresh = (numer + own * denom + penalty * anchor) / (denom + penalty)
    return jnp.where(iota(own.shape, 1) < 2 * DIRS, 0.5 * (own + fresh), 0.0)


def model_kernel(
    offs_hbm, place_hbm, lmn_hbm, flux_hbm, map_hbm, order_hbm, penalty_hbm,
    model_ref, own_ref, table_ref, gains_ref, pred_ref, den_ref, weight_ref,
    offs_ref, xyz_ref, lmn_ref, flux_ref, map_ref, order_ref, penalty_ref, sky_ref, part_ref, sems,
):
    pairs = [
        (map_hbm, map_ref), (lmn_hbm, lmn_ref), (flux_hbm, flux_ref),
        (offs_hbm, offs_ref), (place_hbm, xyz_ref), (penalty_hbm, penalty_ref), (order_hbm, order_ref),
    ]
    copies = [pltpu.make_async_copy(a, b, sems.at[n]) for n, (a, b) in enumerate(pairs)]
    for copy in copies:
        copy.start()
    device = lax.axis_index("stcol")
    scale = 1.0 + 0.5 * lax.axis_index("freq").astype(F32) / CHANNELS
    for copy in copies:
        copy.wait()
    lane = iota((1, LANES), 1)
    weight = jnp.ones((1, LANES), F32)
    for k in range(DIRS):
        weight = jnp.where((lane == k) | (lane == DIRS + k), penalty_ref[0, k], weight)
    weight_ref[...] = weight
    offs = offs_ref[...]
    rows = [1.0 + offs[0:DIRS, :], offs[DIRS : 2 * DIRS, :]] + [xyz_ref[c] for c in range(3)]
    pieces = split3(jnp.concatenate(rows + [jnp.zeros((5, STATIONS), F32)], axis=0))
    place = station_at(iota((STATIONS, STATIONS), 0))
    moved = chosen(pieces, as_table(place == iota((STATIONS, STATIONS), 1)))
    gains_ref[...] = moved[0 : 2 * DIRS, :]
    column = iota((STATIONS, STATIONS), 0)
    column = ((((column >> 3) & 31) ^ LEAD) << 4) + ((column >> 8) << 3) + (column & 7)
    order = order_ref[...]
    digits = jnp.concatenate([order >> 3, order & 7, jnp.zeros((6, STATIONS), jnp.int32)], axis=0).astype(F32)
    digits = dot_nt(digits.astype(BF16), as_table(column == iota((STATIONS, STATIONS), 1)))
    order = (8.0 * digits[0:1, :] + digits[1:2, :]).astype(jnp.int32)
    table_ref[...] = as_table(place == order)
    mine = as_table(iota((ROWS, STATIONS), 1) == row_station((ROWS, STATIONS), 0, device))
    own = sum(dot_nt(mine, piece) for piece in pieces[::-1])
    own = jnp.concatenate([own, jnp.zeros((ROWS, LANES - own.shape[1]), F32)], axis=1)
    own_xyz = [scale * own[:, 2 * DIRS + c : 2 * DIRS + c + 1] for c in range(3)]
    own_ref[...] = jnp.where(iota(own.shape, 1) < 2 * DIRS, own, 0.0)
    count = DIRS * SRC
    member = map_ref[...] == iota((DIRS, count), 0)
    member_f = jnp.where(member, 1.0, 0.0)
    blocks = count // LANES
    stacked = jnp.concatenate([member_f[:, b * LANES : (b + 1) * LANES] for b in range(blocks)], axis=0)
    ahead = as_table(iota((LANES, LANES), 0) <= iota((LANES, LANES), 1))
    running = dot(stacked.astype(BF16), ahead)
    carried = jnp.zeros((DIRS, 1), F32)
    ranks = []
    for b in range(blocks):
        here = running[b * DIRS : (b + 1) * DIRS, :] + carried
        ranks.append(jnp.sum(here * member_f[:, b * LANES : (b + 1) * LANES], axis=0, keepdims=True))
        carried = here[:, LANES - 1 : LANES]
    rank = jnp.concatenate(ranks, axis=1) - 1.0
    slots = as_table(iota((SRC, count), 0) == rank.astype(jnp.int32))
    values = [lmn_ref[0:1, :], lmn_ref[1:2, :], lmn_ref[2:3, :], flux_ref[...]]
    pieces = [[], [], []]
    for value in values:
        for s, piece in enumerate(split3(value)):
            pieces[s].append(piece.astype(F32) * member_f)
    pieces = [jnp.concatenate(p, axis=0).astype(BF16) for p in pieces]
    along = chosen(pieces, slots)
    down = dot_nt(slots, pieces[2]) + dot_nt(slots, pieces[1]) + dot_nt(slots, pieces[0])
    sky_ref[...] = jnp.concatenate([along, along], axis=1)
    part_ref[...] = down
    xyz = [scale * moved[2 * DIRS + c : 2 * DIRS + c + 1, :] for c in range(3)]
    kept = station_at(iota((ROWS, STATIONS), 1)) != row_station((ROWS, STATIONS), 0, device)
    half = iota((1, LANES), 1) < SRC
    shift_real = jnp.where(half, 0.0, 0.25)
    shift_imag = jnp.where(half, 0.25, 0.5)
    for k in range(DIRS):
        column = [part_ref[:, c * DIRS + k : c * DIRS + k + 1] for c in range(3)]
        turns = wrapped(xyz[0] * column[0] + xyz[1] * column[1] + xyz[2] * column[2])
        wave = jnp.concatenate([cos_turns(turns), sin_turns(turns)], axis=0)
        wave_high, wave_low = split2(wave)
        row = [sky_ref[c * DIRS + k : c * DIRS + k + 1, :] for c in range(4)]
        turns = wrapped(own_xyz[0] * row[0] + own_xyz[1] * row[1] + own_xyz[2] * row[2])
        near = jnp.concatenate([cos_turns(wrapped(turns - shift_real)), cos_turns(wrapped(turns - shift_imag))], axis=0)
        near_high, near_low = split2(near * row[3])
        model = dot(near_high, wave_low) + dot(near_low, wave_high) + dot(near_high, wave_high)
        model_ref[k, 0:ROWS, :] = jnp.where(kept, model[0:ROWS, :], 0.0)
        model_ref[k, ROWS : 2 * ROWS, :] = jnp.where(kept, model[ROWS:, :], 0.0)
    for a in range(REPS):
        rows = slice(a * OWN, (a + 1) * OWN)
        pred_real, pred_imag, denom = predict(model_ref, gains_ref, own_ref[rows, :], a * OWN)
        pred_ref[rows, :] = pred_real
        pred_ref[ROWS + a * OWN : ROWS + (a + 1) * OWN, :] = pred_imag
        den_ref[rows, :] = denom


def channel_fit(near_ref, far_ref):
    channel = lax.axis_index("freq")
    total = None
    for d in range(CHANNELS // 2):
        other = channel ^ (2 * d)
        for tiles_ref, source in ((near_ref, other), (far_ref, other ^ 1)):
            part = channel_weight(channel, source) * tiles_ref[d]
            total = part if total is None else total + part
    return unpacked(total)


def sums(model_ref, vis_ref, tiles_ref, own_ref, numer_ref, den_ref, along_ref, part_ref):
    turned = jnp.transpose(tiles_ref[...])
    numer_ref[...], den_ref[...] = row_sums(model_ref, vis_ref, turned, own_ref[...], 0, along_ref, part_ref)


def first_kernel(
    tiles_ref, table_ref, model_ref, gains_ref, pred_ref, den_ref, own_ref, penalty_ref, vis_ref, state_ref, send_ref, part_ref
):
    turned = jnp.transpose(tiles_ref[...])
    pieces = split3(jnp.concatenate([turned[0 : 2 * ROWS, :], turned[2 * ROWS :, :]], axis=1))
    vis_ref[...] = chosen(pieces, table_ref[...])
    for a in range(REPS):
        rows = slice(a * OWN, (a + 1) * OWN)
        lower = slice(ROWS + a * OWN, ROWS + (a + 1) * OWN)
        resid_real = [vis_ref[rows, pieces_of(t)] - pred_ref[rows, pieces_of(t)] for t in range(4)]
        resid_imag = [vis_ref[lower, pieces_of(t)] - pred_ref[lower, pieces_of(t)] for t in range(4)]
        correlate(resid_real, resid_imag, lambda k, t: products(model_ref, gains_ref, a * OWN, k, pieces_of(t)), part_ref)
        total = [[jnp.sum(part_ref[r, k], axis=1, keepdims=True) for k in range(DIRS)] for r in range(2)]
        numer = by_lane(lambda k: total[0][k], lambda k: total[1][k], OWN)
        own = own_ref[rows, :]
        state_ref[rows, :] = updated(numer, den_ref[rows, :], own, own, penalty_ref[...])
    send_ref[...] = packed(state_ref[...])


def second_kernel(
    model_ref, vis_ref, tiles_ref, own_ref, anchor_ref, penalty_ref, state_ref, send_ref, along_ref, part_ref
):
    turned = jnp.transpose(tiles_ref[...])
    own = own_ref[...]
    numer, denom = row_sums(model_ref, vis_ref, turned, own, 0, along_ref, part_ref)
    state = updated(numer, denom, own, anchor_ref[...], penalty_ref[...])
    state_ref[...] = state
    send_ref[...] = packed(state)


def anchor_kernel(numer_ref, den_ref, near_ref, far_ref, own_ref, penalty_ref, state_ref, anchor_ref, dual_ref, send_ref):
    own = own_ref[...]
    cons = channel_fit(near_ref, far_ref)
    dual = own - cons
    anchor = cons - dual
    state = updated(numer_ref[...], den_ref[...], own, anchor, penalty_ref[...])
    state_ref[...] = state
    send_ref[...] = packed(state)
    anchor_ref[...] = anchor
    dual_ref[...] = dual


def by_direction(state):
    filled = jnp.concatenate([state, jnp.zeros((LANES - OWN, LANES), F32)], axis=0)
    return jnp.transpose(filled)[0 : 2 * DIRS, 0:OWN]


def fourth_kernel(
    model_ref, vis_ref, tiles_ref, own_ref, anchor_ref, dual_ref, penalty_ref, state_ref, send_ref, along_ref, part_ref
):
    start = pl.multiple_of(rep_of(lax.axis_index("stcol")) * OWN, OWN)
    rows = pl.ds(start, OWN)
    own = own_ref[rows, :]
    turned = jnp.transpose(tiles_ref[...])
    numer, denom = row_sums(model_ref, vis_ref, turned, own, start, along_ref, part_ref)
    state = updated(numer, denom, own, anchor_ref[rows, :], penalty_ref[...])
    state_ref[...] = state
    send_ref[...] = packed(state + dual_ref[rows, :])


def last_kernel(tiles_ref, state_ref, out_ref, cons_ref):
    out_ref[...] = by_direction(state_ref[...])
    channel = lax.axis_index("freq")
    total = basis_product(channel, HEAD) * tiles_ref[0]
    for f in range(1, CHANNELS):
        total = total + basis_product(channel, f ^ HEAD) * tiles_ref[f]
    cons_ref[...] = by_direction(unpacked(total))


def called(kernel, outs, scratch=(), name=None, in_specs=None):
    return pl.pallas_call(
        kernel,
        out_shape=[jax.ShapeDtypeStruct(*o) for o in outs],
        scratch_shapes=[pltpu.VMEM(*o) if isinstance(o, tuple) else o for o in scratch],
        compiler_params=pltpu.CompilerParams(vmem_limit_bytes=32 * 1024 * 1024),
        name=name,
        **({} if in_specs is None else {"in_specs": in_specs}),
    )


def held(x):
    return pltpu.with_memory_space_constraint(x, pltpu.HBM)


def to_all(tile, axis, count, groups=None):
    tiles = jnp.broadcast_to(tile, (count, *tile.shape))
    return lax.all_to_all(tiles, axis, 0, 0, tiled=True, axis_index_groups=groups)


def around(tile):
    return [tile] + [
        lax.ppermute(tile, "freq", [(i, i ^ (2 * d)) for i in range(CHANNELS)]) for d in range(1, CHANNELS // 2)
    ]


def both_cores(tiles):
    near = jnp.stack(tiles)
    return near, lax.ppermute(near, "freq", [(i, i ^ 1) for i in range(CHANNELS)])


def to_members(tile):
    members = [e ^ FRONT for e in range(MEMBERS)]
    groups = [[(e >> 2) * 8 + 4 * m + (e & 3) for e in members] for m in range(REPS)]
    return to_all(tile, "stcol", MEMBERS, groups).reshape(LANES, LANES)


def on_device(visibilities, positions, source_lmn, source_flux, cluster_map, station_order, penalty, offsets):
    hbm = pl.BlockSpec(memory_space=pltpu.HBM)
    model_out = ((DIRS, 2 * ROWS, STATIONS), F32)
    along = ((DIRS, 2 * OWN, STATIONS), F32)
    part = ((3, DIRS, OWN, LANES), F32)
    parts = ((3, DIRS, ROWS, LANES), F32)
    vis_out = ((2 * ROWS, STATIONS), F32)
    state_out = ((ROWS, LANES), F32)
    send_out = ((ROWS // 4, LANES), F32)
    flat_out = ((2 * DIRS, OWN), F32)
    gains_out = ((2 * DIRS, STATIONS), F32)
    (tiles,) = called(
        turn_kernel,
        [((STATIONS // OWN, 8, LANES), F32)],
        [((2 * OWN, 1, STATIONS), F32), pltpu.SemaphoreType.DMA],
        "turn",
        [hbm],
    )(held(visibilities.reshape(2 * OWN, 1, STATIONS)))
    slots = [s ^ LEAD for s in range(STATIONS // OWN)]
    tiles = lax.all_to_all(tiles, "stcol", 0, 0, tiled=True, axis_index_groups=[slots]).reshape(STATIONS // 2, LANES)
    count = DIRS * SRC
    model, own, table, gains, pred, den, pen = called(
        model_kernel,
        [model_out, state_out, ((STATIONS, STATIONS), BF16), gains_out, vis_out, state_out, ((1, LANES), F32)],
        [
            gains_out, ((3, 1, STATIONS), F32), ((3, count), F32), ((1, count), F32), ((1, count), jnp.int32),
            ((1, STATIONS), jnp.int32), pltpu.SMEM((1, DIRS), F32), ((4 * DIRS, 2 * SRC), F32), ((SRC, 4 * DIRS), F32),
            pltpu.SemaphoreType.DMA((7,)),
        ],
        "models",
        [hbm] * 7,
    )(
        held(offsets.reshape(2 * DIRS, STATIONS)), held(positions), held(source_lmn), held(source_flux.reshape(1, count)),
        held(cluster_map.reshape(1, count)), held(station_order.reshape(1, STATIONS)), held(penalty.reshape(1, DIRS)),
    )
    vis, state, send = called(first_kernel, [vis_out, state_out, send_out], [((2, DIRS, OWN, LANES), F32)], "pass_one")(
        tiles, table, model, gains, pred, den, own, pen
    )
    got = to_members(send)
    state, send = called(second_kernel, [state_out, send_out], [model_out, parts], "pass_two")(
        model, vis, got, state, own, pen
    )
    tiles = around(send)
    got = to_members(send)
    numer, den = called(sums, [state_out, state_out], [model_out, parts], "pass_three")(model, vis, got, state)
    near, far = both_cores(lax.optimization_barrier((*tiles, got))[:-1])
    state, anchor, dual, send = called(anchor_kernel, [state_out, state_out, state_out, send_out], name="update_three")(
        numer, den, near, far, state, pen
    )
    got = to_members(send)
    state, send = called(fourth_kernel, [((OWN, LANES), F32), ((4, LANES), F32)], [along, part], "pass_four")(
        model, vis, got, state, anchor, dual, pen
    )
    out, cons = called(last_kernel, [flat_out, flat_out], name="consensus")(to_all(send, "freq", CHANNELS, [[f ^ HEAD for f in range(CHANNELS)]]), state)
    shape = (2, 1, DIRS, OWN)
    return out.reshape(shape), cons.reshape(shape)


def solution(mesh):
    in_specs = (
        P(None, "freq", "stcol", None, None),
        P(),
        P(),
        P(),
        P(),
        P(),
        P(),
        P(None, "freq", None, None),
    )
    out_specs = (P(None, "freq", None, "stcol"), P(None, "freq", None, "stcol"))
    return jax.shard_map(
        on_device, mesh=mesh, in_specs=in_specs, out_specs=out_specs, check_vma=False
    )
```

```python
import math

import jax
import jax.numpy as jnp
import numpy as np
from jax import lax
from jax.experimental import pallas as pl
from jax.experimental.pallas import tpu as pltpu
from jax.sharding import PartitionSpec as P

STATIONS = 512
DIRS = 16
SRC = 64
CHANNELS = 8
OWN = 16
REPS = 2
ROWS = REPS * OWN
MEMBERS = STATIONS // ROWS
LANES = 128
FRONT = 10
LEAD = 31
HEAD = 4
F32 = jnp.float32
BF16 = jnp.bfloat16

COS_TERMS = None
SIN_TERMS = None


def fit_terms():
    nodes = np.cos(np.pi * (np.arange(400) + 0.5) / 400)
    u = 0.125 * (nodes + 1.0)
    r = np.sqrt(u)
    cheb = np.polynomial.chebyshev
    poly = np.polynomial.polynomial

    def terms(values, degree):
        series = cheb.cheb2poly(cheb.chebfit(nodes, values, degree))
        out = np.zeros(1)
        for c in series[::-1]:
            out = poly.polyadd(poly.polymul(out, [-1.0, 8.0]), [c])
        return [float(np.float32(c)) for c in out[: degree + 1]]

    return terms(np.cos(2 * np.pi * r), 6), terms(np.sin(2 * np.pi * r) / r, 6)


COS_TERMS, SIN_TERMS = fit_terms()


def basis_table():
    centre = (np.arange(CHANNELS) - 0.5 * (CHANNELS - 1)) / CHANNELS
    columns = [np.ones_like(centre), centre, centre * centre]
    finished = []
    for column in columns:
        for before in finished:
            column = column - np.sum(column * before) * before
        finished.append(column / np.sqrt(np.sum(column * column)))
    return np.stack(finished, axis=1)


BASIS = basis_table()


def basis_row(channel):
    centre = (np.arange(CHANNELS) - 0.5 * (CHANNELS - 1)) / CHANNELS
    square = centre * centre
    flat = BASIS[:, 0]
    lift = float(np.sum(square * flat))
    norm1 = float(np.sqrt(np.sum(centre * centre)))
    norm2 = float(np.sqrt(np.sum((square - lift * flat) ** 2)))
    x = (channel.astype(F32) - 0.5 * (CHANNELS - 1)) * (1.0 / CHANNELS)
    return (float(flat[0]), x * (1.0 / norm1), (x * x - lift * float(flat[0])) * (1.0 / norm2))


def channel_weight(channel, source):
    return sum(a * b for a, b in zip(basis_row(channel), basis_row(source)))


def basis_product(channel, source):
    return sum(a * float(b) for a, b in zip(basis_row(channel), BASIS[source]))


def horner(u, terms):
    out = jnp.full_like(u, terms[-1])
    for c in terms[-2::-1]:
        out = out * u + c
    return out


def wrapped(turns):
    return turns - ((turns + 12582912.0) - 12582912.0)


def cos_turns(r):
    return horner(r * r, COS_TERMS)


def sin_turns(r):
    return r * horner(r * r, SIN_TERMS)


def split2(x):
    high = x.astype(BF16)
    return high, (x - high.astype(F32)).astype(BF16)


def split3(x):
    high = x.astype(BF16)
    rest = x - high.astype(F32)
    mid = rest.astype(BF16)
    return high, mid, (rest - mid.astype(F32)).astype(BF16)


def dot(a, b):
    return lax.dot_general(a, b, (((1,), (0,)), ((), ())), preferred_element_type=F32)


def dot_nt(a, b):
    return lax.dot_general(a, b, (((1,), (1,)), ((), ())), preferred_element_type=F32)


def chosen(pieces, table):
    return dot_nt(pieces[2], table) + dot_nt(pieces[1], table) + dot_nt(pieces[0], table)


def iota(shape, dim):
    return lax.broadcasted_iota(jnp.int32, shape, dim)


def as_table(cond):
    return jnp.where(cond, jnp.ones(cond.shape, F32), jnp.zeros(cond.shape, F32)).astype(BF16)


def station_at(place):
    member = ((place >> 3) & 15) ^ FRONT
    return ((member >> 2) << 7) + ((place >> 8) << 6) + ((member & 3) << 4) + (((place >> 7) & 1) << 3) + (place & 7)


def row_station(shape, dim, device):
    row = iota(shape, dim)
    return ((row >> 4) << 6) + (row & 15) + ((device >> 3) << 7) + ((device & 3) << 4)


def rep_of(device):
    return (device & 7) >> 2


def packed(state):
    n = state.shape[0] // 4
    out = state[0:n, :]
    for a in range(1, 4):
        out = out + pltpu.roll(state, 32 * a, 1)[n * a : n * a + n, :]
    return out


def unpacked(tile):
    rows = [tile] + [pltpu.roll(tile, LANES - 32 * a, 1) for a in range(1, 4)]
    both = jnp.concatenate(rows, axis=0)
    return jnp.where(iota(both.shape, 1) < 2 * DIRS, both, 0.0)


def turn_kernel(vis_hbm, tiles_ref, vis_ref, sem):
    copy = pltpu.make_async_copy(vis_hbm, vis_ref, sem)
    copy.start()
    copy.wait()
    lane = iota((8, LANES), 1)
    for x in range(4):
        parts = [vis_ref[r * 8 : (r + 1) * 8, 0, x * LANES : (x + 1) * LANES] for r in range(4)]
        for b in range(4):
            tile = jnp.zeros((8, LANES), F32)
            for half in range(2):
                for r in range(2):
                    for a in range(REPS):
                        to = half * 64 + r * ROWS + a * OWN
                        moved = pltpu.roll(parts[2 * r + half], (to - (64 * a + 16 * b)) % LANES, 1)
                        tile = jnp.where((lane >> 4) == (to >> 4), moved, tile)
            for a in range(REPS):
                tiles_ref[(x * 8 + 4 * a + b) ^ LEAD] = tile


def products(model_ref, gains_ref, start, k, lanes=slice(None)):
    half = model_ref.shape[1] // 2
    model_real = model_ref[k, pl.ds(start, OWN), lanes]
    model_imag = model_ref[k, pl.ds(start + half, OWN), lanes]
    col_real = gains_ref[k : k + 1, lanes]
    col_imag = gains_ref[DIRS + k : DIRS + k + 1, lanes]
    return model_real * col_real + model_imag * col_imag, model_imag * col_real - model_real * col_imag


def predict(model_ref, gains_ref, own, start):
    pred_real = jnp.zeros((OWN, STATIONS), F32)
    pred_imag = jnp.zeros((OWN, STATIONS), F32)
    lane = iota((OWN, LANES), 1)
    denom = jnp.zeros((OWN, LANES), F32)
    for k in range(DIRS):
        along_real, along_imag = products(model_ref, gains_ref, start, k)
        row_real = own[:, k : k + 1]
        row_imag = own[:, DIRS + k : DIRS + k + 1]
        pred_real = pred_real + (row_real * along_real - row_imag * along_imag)
        pred_imag = pred_imag + (row_real * along_imag + row_imag * along_real)
        den = jnp.sum(along_real * along_real + along_imag * along_imag, axis=1, keepdims=True)
        denom = jnp.where((lane == k) | (lane == DIRS + k), den, denom)
    return pred_real, pred_imag, denom


def lane_sums(part_ref):
    shape = part_ref.shape
    high, low = split2(part_ref[...].reshape(-1, LANES))
    ones = jnp.ones((LANES, LANES), BF16)
    return (dot(low, ones) + dot(high, ones)).reshape(shape)


def by_lane(real, imag, rows):
    lane = iota((rows, LANES), 1)
    out = jnp.zeros((rows, LANES), F32)
    for k in range(DIRS):
        out = jnp.where(lane == k, real(k), jnp.where(lane == DIRS + k, imag(k), out))
    return out


def pieces_of(t):
    return slice(t * LANES, (t + 1) * LANES)


def row_sums(model_ref, vis_ref, turned, own, start, along_ref, part_ref):
    n = own.shape[0]
    real_rows, imag_rows = pl.ds(start, n), pl.ds(start + ROWS, n)
    pred_real = [jnp.zeros((n, LANES), F32)] * 4
    pred_imag = [jnp.zeros((n, LANES), F32)] * 4
    for k in range(DIRS):
        row_real = jnp.broadcast_to(own[:, k : k + 1], (n, LANES))
        row_imag = jnp.broadcast_to(own[:, DIRS + k : DIRS + k + 1], (n, LANES))
        squares = None
        for t in range(4):
            col_real = turned[32 * t + k : 32 * t + k + 1, :]
            col_imag = turned[32 * t + DIRS + k : 32 * t + DIRS + k + 1, :]
            model_real = model_ref[k, real_rows, pieces_of(t)]
            model_imag = model_ref[k, imag_rows, pieces_of(t)]
            along_real = model_real * col_real + model_imag * col_imag
            along_imag = model_imag * col_real - model_real * col_imag
            along_ref[k, 0:n, pieces_of(t)] = along_real
            along_ref[k, n : 2 * n, pieces_of(t)] = along_imag
            pred_real[t] = pred_real[t] + (row_real * along_real - row_imag * along_imag)
            pred_imag[t] = pred_imag[t] + (row_real * along_imag + row_imag * along_real)
            square = along_real * along_real + along_imag * along_imag
            squares = square if squares is None else squares + square
        part_ref[2, k] = squares
    resid_real = [vis_ref[real_rows, pieces_of(t)] - pred_real[t] for t in range(4)]
    resid_imag = [vis_ref[imag_rows, pieces_of(t)] - pred_imag[t] for t in range(4)]
    correlate(resid_real, resid_imag, lambda k, t: (along_ref[k, 0:n, pieces_of(t)], along_ref[k, n : 2 * n, pieces_of(t)]), part_ref)
    sums = lane_sums(part_ref)
    return by_lane(lambda k: sums[0, k], lambda k: sums[1, k], n), by_lane(lambda k: sums[2, k], lambda k: sums[2, k], n)


def correlate(resid_real, resid_imag, along, part_ref):
    for k in range(DIRS):
        real = imag = None
        for t in range(4):
            along_real, along_imag = along(k, t)
            u = resid_real[t] * along_real + resid_imag[t] * along_imag
            v = resid_imag[t] * along_real - resid_real[t] * along_imag
            real = u if real is None else real + u
            imag = v if imag is None else imag + v
        part_ref[0, k] = real
        part_ref[1, k] = imag


def updated(numer, denom, own, anchor, penalty):
    fresh = (numer + own * denom + penalty * anchor) / (denom + penalty)
    return jnp.where(iota(own.shape, 1) < 2 * DIRS, 0.5 * (own + fresh), 0.0)


def model_kernel(
    offs_hbm, place_hbm, lmn_hbm, flux_hbm, map_hbm, order_hbm, penalty_hbm,
    model_ref, own_ref, table_ref, gains_ref, pred_ref, den_ref, weight_ref,
    offs_ref, xyz_ref, lmn_ref, flux_ref, map_ref, order_ref, penalty_ref, sky_ref, part_ref, sems,
):
    pairs = [
        (map_hbm, map_ref), (lmn_hbm, lmn_ref), (flux_hbm, flux_ref),
        (offs_hbm, offs_ref), (place_hbm, xyz_ref), (penalty_hbm, penalty_ref), (order_hbm, order_ref),
    ]
    copies = [pltpu.make_async_copy(a, b, sems.at[n]) for n, (a, b) in enumerate(pairs)]
    for copy in copies:
        copy.start()
    device = lax.axis_index("stcol")
    scale = 1.0 + 0.5 * lax.axis_index("freq").astype(F32) / CHANNELS
    place = station_at(iota((STATIONS, STATIONS), 0))
    placing = as_table(place == iota((STATIONS, STATIONS), 1))
    column = iota((STATIONS, STATIONS), 0)
    column = ((((column >> 3) & 31) ^ LEAD) << 4) + ((column >> 8) << 3) + (column & 7)
    ordering = as_table(column == iota((STATIONS, STATIONS), 1))
    mine = as_table(iota((ROWS, STATIONS), 1) == row_station((ROWS, STATIONS), 0, device))
    ahead = as_table(iota((LANES, LANES), 0) <= iota((LANES, LANES), 1))
    for copy in copies:
        copy.wait()
    lane = iota((1, LANES), 1)
    weight = jnp.ones((1, LANES), F32)
    for k in range(DIRS):
        weight = jnp.where((lane == k) | (lane == DIRS + k), penalty_ref[0, k], weight)
    weight_ref[...] = weight
    offs = offs_ref[...]
    rows = [1.0 + offs[0:DIRS, :], offs[DIRS : 2 * DIRS, :]] + [xyz_ref[c] for c in range(3)]
    pieces = split3(jnp.concatenate(rows + [jnp.zeros((5, STATIONS), F32)], axis=0))
    moved = chosen(pieces, placing)
    gains_ref[...] = moved[0 : 2 * DIRS, :]
    order = order_ref[...]
    digits = jnp.concatenate([order >> 3, order & 7, jnp.zeros((6, STATIONS), jnp.int32)], axis=0).astype(F32)
    digits = dot_nt(digits.astype(BF16), ordering)
    order = (8.0 * digits[0:1, :] + digits[1:2, :]).astype(jnp.int32)
    table_ref[...] = as_table(place == order)
    own = sum(dot_nt(mine, piece) for piece in pieces[::-1])
    own = jnp.concatenate([own, jnp.zeros((ROWS, LANES - own.shape[1]), F32)], axis=1)
    own_xyz = [scale * own[:, 2 * DIRS + c : 2 * DIRS + c + 1] for c in range(3)]
    own_ref[...] = jnp.where(iota(own.shape, 1) < 2 * DIRS, own, 0.0)
    count = DIRS * SRC
    member = map_ref[...] == iota((DIRS, count), 0)
    member_f = jnp.where(member, 1.0, 0.0)
    blocks = count // LANES
    stacked = jnp.concatenate([member_f[:, b * LANES : (b + 1) * LANES] for b in range(blocks)], axis=0)
    running = dot(stacked.astype(BF16), ahead)
    carried = jnp.zeros((DIRS, 1), F32)
    ranks = []
    for b in range(blocks):
        here = running[b * DIRS : (b + 1) * DIRS, :] + carried
        ranks.append(jnp.sum(here * member_f[:, b * LANES : (b + 1) * LANES], axis=0, keepdims=True))
        carried = here[:, LANES - 1 : LANES]
    rank = jnp.concatenate(ranks, axis=1) - 1.0
    slots = as_table(iota((SRC, count), 0) == rank.astype(jnp.int32))
    values = [lmn_ref[0:1, :], lmn_ref[1:2, :], lmn_ref[2:3, :], flux_ref[...]]
    pieces = [[], [], []]
    for value in values:
        for s, piece in enumerate(split3(value)):
            pieces[s].append(piece.astype(F32) * member_f)
    pieces = [jnp.concatenate(p, axis=0).astype(BF16) for p in pieces]
    along = chosen(pieces, slots)
    down = dot_nt(slots, pieces[2]) + dot_nt(slots, pieces[1]) + dot_nt(slots, pieces[0])
    sky_ref[...] = jnp.concatenate([along, along], axis=1)
    part_ref[...] = down
    xyz = [scale * moved[2 * DIRS + c : 2 * DIRS + c + 1, :] for c in range(3)]
    kept = station_at(iota((ROWS, STATIONS), 1)) != row_station((ROWS, STATIONS), 0, device)
    half = iota((1, LANES), 1) < SRC
    shift_real = jnp.where(half, 0.0, 0.25)
    shift_imag = jnp.where(half, 0.25, 0.5)
    for k in range(DIRS):
        column = [part_ref[:, c * DIRS + k : c * DIRS + k + 1] for c in range(3)]
        turns = wrapped(xyz[0] * column[0] + xyz[1] * column[1] + xyz[2] * column[2])
        wave = jnp.concatenate([cos_turns(turns), sin_turns(turns)], axis=0)
        wave_high, wave_low = split2(wave)
        row = [sky_ref[c * DIRS + k : c * DIRS + k + 1, :] for c in range(4)]
        turns = wrapped(own_xyz[0] * row[0] + own_xyz[1] * row[1] + own_xyz[2] * row[2])
        near = jnp.concatenate([cos_turns(wrapped(turns - shift_real)), cos_turns(wrapped(turns - shift_imag))], axis=0)
        near_high, near_low = split2(near * row[3])
        model = dot(near_high, wave_low) + dot(near_low, wave_high) + dot(near_high, wave_high)
        model_ref[k, 0:ROWS, :] = jnp.where(kept, model[0:ROWS, :], 0.0)
        model_ref[k, ROWS : 2 * ROWS, :] = jnp.where(kept, model[ROWS:, :], 0.0)
    for a in range(REPS):
        rows = slice(a * OWN, (a + 1) * OWN)
        pred_real, pred_imag, denom = predict(model_ref, gains_ref, own_ref[rows, :], a * OWN)
        pred_ref[rows, :] = pred_real
        pred_ref[ROWS + a * OWN : ROWS + (a + 1) * OWN, :] = pred_imag
        den_ref[rows, :] = denom


def channel_fit(near_ref, far_ref):
    channel = lax.axis_index("freq")
    total = None
    for d in range(CHANNELS // 2):
        other = channel ^ (2 * d)
        for tiles_ref, source in ((near_ref, other), (far_ref, other ^ 1)):
            part = channel_weight(channel, source) * tiles_ref[d]
            total = part if total is None else total + part
    return unpacked(total)


def sums(model_ref, vis_ref, tiles_ref, own_ref, numer_ref, den_ref, along_ref, part_ref):
    turned = jnp.transpose(tiles_ref[...])
    numer_ref[...], den_ref[...] = row_sums(model_ref, vis_ref, turned, own_ref[...], 0, along_ref, part_ref)


def first_kernel(
    tiles_ref, table_ref, model_ref, gains_ref, pred_ref, den_ref, own_ref, penalty_ref, vis_ref, state_ref, send_ref, part_ref
):
    turned = jnp.transpose(tiles_ref[...])
    pieces = split3(jnp.concatenate([turned[0 : 2 * ROWS, :], turned[2 * ROWS :, :]], axis=1))
    vis_ref[...] = chosen(pieces, table_ref[...])
    for a in range(REPS):
        rows = slice(a * OWN, (a + 1) * OWN)
        lower = slice(ROWS + a * OWN, ROWS + (a + 1) * OWN)
        resid_real = [vis_ref[rows, pieces_of(t)] - pred_ref[rows, pieces_of(t)] for t in range(4)]
        resid_imag = [vis_ref[lower, pieces_of(t)] - pred_ref[lower, pieces_of(t)] for t in range(4)]
        correlate(resid_real, resid_imag, lambda k, t: products(model_ref, gains_ref, a * OWN, k, pieces_of(t)), part_ref)
        total = [[jnp.sum(part_ref[r, k], axis=1, keepdims=True) for k in range(DIRS)] for r in range(2)]
        numer = by_lane(lambda k: total[0][k], lambda k: total[1][k], OWN)
        own = own_ref[rows, :]
        state_ref[rows, :] = updated(numer, den_ref[rows, :], own, own, penalty_ref[...])
    send_ref[...] = packed(state_ref[...])


def second_kernel(
    model_ref, vis_ref, tiles_ref, own_ref, anchor_ref, penalty_ref, state_ref, send_ref, along_ref, part_ref
):
    turned = jnp.transpose(tiles_ref[...])
    own = own_ref[...]
    numer, denom = row_sums(model_ref, vis_ref, turned, own, 0, along_ref, part_ref)
    state = updated(numer, denom, own, anchor_ref[...], penalty_ref[...])
    state_ref[...] = state
    send_ref[...] = packed(state)


def anchor_kernel(numer_ref, den_ref, near_ref, far_ref, own_ref, penalty_ref, state_ref, anchor_ref, dual_ref, send_ref):
    own = own_ref[...]
    cons = channel_fit(near_ref, far_ref)
    dual = own - cons
    anchor = cons - dual
    state = updated(numer_ref[...], den_ref[...], own, anchor, penalty_ref[...])
    state_ref[...] = state
    send_ref[...] = packed(state)
    anchor_ref[...] = anchor
    dual_ref[...] = dual


def by_direction(state):
    filled = jnp.concatenate([state, jnp.zeros((LANES - OWN, LANES), F32)], axis=0)
    return jnp.transpose(filled)[0 : 2 * DIRS, 0:OWN]


def fourth_kernel(
    model_ref, vis_ref, tiles_ref, own_ref, anchor_ref, dual_ref, penalty_ref, state_ref, send_ref, along_ref, part_ref
):
    start = pl.multiple_of(rep_of(lax.axis_index("stcol")) * OWN, OWN)
    rows = pl.ds(start, OWN)
    own = own_ref[rows, :]
    turned = jnp.transpose(tiles_ref[...])
    numer, denom = row_sums(model_ref, vis_ref, turned, own, start, along_ref, part_ref)
    state = updated(numer, denom, own, anchor_ref[rows, :], penalty_ref[...])
    state_ref[...] = state
    send_ref[...] = packed(state + dual_ref[rows, :])


def last_kernel(tiles_ref, state_ref, out_ref, cons_ref):
    out_ref[...] = by_direction(state_ref[...])
    channel = lax.axis_index("freq")
    total = basis_product(channel, HEAD) * tiles_ref[0]
    for f in range(1, CHANNELS):
        total = total + basis_product(channel, f ^ HEAD) * tiles_ref[f]
    cons_ref[...] = by_direction(unpacked(total))


def called(kernel, outs, scratch=(), name=None, in_specs=None):
    return pl.pallas_call(
        kernel,
        out_shape=[jax.ShapeDtypeStruct(*o) for o in outs],
        scratch_shapes=[pltpu.VMEM(*o) if isinstance(o, tuple) else o for o in scratch],
        compiler_params=pltpu.CompilerParams(vmem_limit_bytes=32 * 1024 * 1024),
        name=name,
        **({} if in_specs is None else {"in_specs": in_specs}),
    )


def held(x):
    return pltpu.with_memory_space_constraint(x, pltpu.HBM)


def to_all(tile, axis, count, groups=None):
    tiles = jnp.broadcast_to(tile, (count, *tile.shape))
    return lax.all_to_all(tiles, axis, 0, 0, tiled=True, axis_index_groups=groups)


def around(tile):
    swaps = {d: lax.ppermute(tile, "freq", [(i, i ^ (2 * d)) for i in range(CHANNELS)]) for d in (1, 3, 2)}
    return [tile, swaps[1], swaps[2], swaps[3]]


def both_cores(tiles):
    near = jnp.stack(tiles)
    return near, lax.ppermute(near, "freq", [(i, i ^ 1) for i in range(CHANNELS)])


def to_members(tile):
    members = [e ^ FRONT for e in range(MEMBERS)]
    groups = [[(e >> 2) * 8 + 4 * m + (e & 3) for e in members] for m in range(REPS)]
    return to_all(tile, "stcol", MEMBERS, groups).reshape(LANES, LANES)


def on_device(visibilities, positions, source_lmn, source_flux, cluster_map, station_order, penalty, offsets):
    hbm = pl.BlockSpec(memory_space=pltpu.HBM)
    model_out = ((DIRS, 2 * ROWS, STATIONS), F32)
    along = ((DIRS, 2 * OWN, STATIONS), F32)
    part = ((3, DIRS, OWN, LANES), F32)
    parts = ((3, DIRS, ROWS, LANES), F32)
    vis_out = ((2 * ROWS, STATIONS), F32)
    state_out = ((ROWS, LANES), F32)
    send_out = ((ROWS // 4, LANES), F32)
    flat_out = ((2 * DIRS, OWN), F32)
    gains_out = ((2 * DIRS, STATIONS), F32)
    (tiles,) = called(
        turn_kernel,
        [((STATIONS // OWN, 8, LANES), F32)],
        [((2 * OWN, 1, STATIONS), F32), pltpu.SemaphoreType.DMA],
        "turn",
        [hbm],
    )(held(visibilities.reshape(2 * OWN, 1, STATIONS)))
    slots = [s ^ LEAD for s in range(STATIONS // OWN)]
    tiles = lax.all_to_all(tiles, "stcol", 0, 0, tiled=True, axis_index_groups=[slots]).reshape(STATIONS // 2, LANES)
    count = DIRS * SRC
    model, own, table, gains, pred, den, pen = called(
        model_kernel,
        [model_out, state_out, ((STATIONS, STATIONS), BF16), gains_out, vis_out, state_out, ((1, LANES), F32)],
        [
            gains_out, ((3, 1, STATIONS), F32), ((3, count), F32), ((1, count), F32), ((1, count), jnp.int32),
            ((1, STATIONS), jnp.int32), pltpu.SMEM((1, DIRS), F32), ((4 * DIRS, 2 * SRC), F32), ((SRC, 4 * DIRS), F32),
            pltpu.SemaphoreType.DMA((7,)),
        ],
        "models",
        [hbm] * 7,
    )(
        held(offsets.reshape(2 * DIRS, STATIONS)), held(positions), held(source_lmn), held(source_flux.reshape(1, count)),
        held(cluster_map.reshape(1, count)), held(station_order.reshape(1, STATIONS)), held(penalty.reshape(1, DIRS)),
    )
    vis, state, send = called(first_kernel, [vis_out, state_out, send_out], [((2, DIRS, OWN, LANES), F32)], "pass_one")(
        tiles, table, model, gains, pred, den, own, pen
    )
    got = to_members(send)
    state, send = called(second_kernel, [state_out, send_out], [model_out, parts], "pass_two")(
        model, vis, got, state, own, pen
    )
    tiles = around(send)
    got = to_members(send)
    numer, den = called(sums, [state_out, state_out], [model_out, parts], "pass_three")(model, vis, got, state)
    near, far = both_cores(lax.optimization_barrier((*tiles, got))[:-1])
    state, anchor, dual, send = called(anchor_kernel, [state_out, state_out, state_out, send_out], name="update_three")(
        numer, den, near, far, state, pen
    )
    got = to_members(send)
    state, send = called(fourth_kernel, [((OWN, LANES), F32), ((4, LANES), F32)], [along, part], "pass_four")(
        model, vis, got, state, anchor, dual, pen
    )
    out, cons = called(last_kernel, [flat_out, flat_out], name="consensus")(to_all(send, "freq", CHANNELS, [[f ^ HEAD for f in range(CHANNELS)]]), state)
    shape = (2, 1, DIRS, OWN)
    return out.reshape(shape), cons.reshape(shape)


def solution(mesh):
    in_specs = (
        P(None, "freq", "stcol", None, None),
        P(),
        P(),
        P(),
        P(),
        P(),
        P(),
        P(None, "freq", None, None),
    )
    out_specs = (P(None, "freq", None, "stcol"), P(None, "freq", None, "stcol"))
    return jax.shard_map(
        on_device, mesh=mesh, in_specs=in_specs, out_specs=out_specs, check_vma=False
    )
```

```python
import math

import jax
import jax.numpy as jnp
import numpy as np
from jax import lax
from jax.experimental import pallas as pl
from jax.experimental.pallas import tpu as pltpu
from jax.sharding import PartitionSpec as P

STATIONS = 512
DIRS = 16
SRC = 64
CHANNELS = 8
OWN = 16
REPS = 2
ROWS = REPS * OWN
MEMBERS = STATIONS // ROWS
LANES = 128
FRONT = 10
LEAD = 31
HEAD = 4
F32 = jnp.float32
BF16 = jnp.bfloat16

COS_TERMS = None
SIN_TERMS = None


def fit_terms():
    nodes = np.cos(np.pi * (np.arange(400) + 0.5) / 400)
    u = 0.125 * (nodes + 1.0)
    r = np.sqrt(u)
    cheb = np.polynomial.chebyshev
    poly = np.polynomial.polynomial

    def terms(values, degree):
        series = cheb.cheb2poly(cheb.chebfit(nodes, values, degree))
        out = np.zeros(1)
        for c in series[::-1]:
            out = poly.polyadd(poly.polymul(out, [-1.0, 8.0]), [c])
        return [float(np.float32(c)) for c in out[: degree + 1]]

    return terms(np.cos(2 * np.pi * r), 6), terms(np.sin(2 * np.pi * r) / r, 6)


COS_TERMS, SIN_TERMS = fit_terms()


def basis_table():
    centre = (np.arange(CHANNELS) - 0.5 * (CHANNELS - 1)) / CHANNELS
    columns = [np.ones_like(centre), centre, centre * centre]
    finished = []
    for column in columns:
        for before in finished:
            column = column - np.sum(column * before) * before
        finished.append(column / np.sqrt(np.sum(column * column)))
    return np.stack(finished, axis=1)


BASIS = basis_table()


def basis_row(channel):
    centre = (np.arange(CHANNELS) - 0.5 * (CHANNELS - 1)) / CHANNELS
    square = centre * centre
    flat = BASIS[:, 0]
    lift = float(np.sum(square * flat))
    norm1 = float(np.sqrt(np.sum(centre * centre)))
    norm2 = float(np.sqrt(np.sum((square - lift * flat) ** 2)))
    x = (channel.astype(F32) - 0.5 * (CHANNELS - 1)) * (1.0 / CHANNELS)
    return (float(flat[0]), x * (1.0 / norm1), (x * x - lift * float(flat[0])) * (1.0 / norm2))


def channel_weight(channel, source):
    return sum(a * b for a, b in zip(basis_row(channel), basis_row(source)))


def basis_product(channel, source):
    return sum(a * float(b) for a, b in zip(basis_row(channel), BASIS[source]))


def horner(u, terms):
    out = jnp.full_like(u, terms[-1])
    for c in terms[-2::-1]:
        out = out * u + c
    return out


def wrapped(turns):
    return turns - ((turns + 12582912.0) - 12582912.0)


def cos_turns(r):
    return horner(r * r, COS_TERMS)


def sin_turns(r):
    return r * horner(r * r, SIN_TERMS)


def split2(x):
    high = x.astype(BF16)
    return high, (x - high.astype(F32)).astype(BF16)


def split3(x):
    high = x.astype(BF16)
    rest = x - high.astype(F32)
    mid = rest.astype(BF16)
    return high, mid, (rest - mid.astype(F32)).astype(BF16)


def dot(a, b):
    return lax.dot_general(a, b, (((1,), (0,)), ((), ())), preferred_element_type=F32)


def dot_nt(a, b):
    return lax.dot_general(a, b, (((1,), (1,)), ((), ())), preferred_element_type=F32)


def chosen(pieces, table):
    return dot_nt(pieces[2], table) + dot_nt(pieces[1], table) + dot_nt(pieces[0], table)


def iota(shape, dim):
    return lax.broadcasted_iota(jnp.int32, shape, dim)


def as_table(cond):
    return jnp.where(cond, jnp.ones(cond.shape, F32), jnp.zeros(cond.shape, F32)).astype(BF16)


def station_at(place):
    member = ((place >> 3) & 15) ^ FRONT
    return ((member >> 2) << 7) + ((place >> 8) << 6) + ((member & 3) << 4) + (((place >> 7) & 1) << 3) + (place & 7)


def row_station(shape, dim, device):
    row = iota(shape, dim)
    return ((row >> 4) << 6) + (row & 15) + ((device >> 3) << 7) + ((device & 3) << 4)


def rep_of(device):
    return (device & 7) >> 2


def packed(state):
    n = state.shape[0] // 4
    out = state[0:n, :]
    for a in range(1, 4):
        out = out + pltpu.roll(state, 32 * a, 1)[n * a : n * a + n, :]
    return out


def unpacked(tile):
    rows = [tile] + [pltpu.roll(tile, LANES - 32 * a, 1) for a in range(1, 4)]
    both = jnp.concatenate(rows, axis=0)
    return jnp.where(iota(both.shape, 1) < 2 * DIRS, both, 0.0)


def turn_kernel(vis_hbm, tiles_hbm, vis_ref, tiles_ref, sems):
    copy = pltpu.make_async_copy(vis_hbm, vis_ref, sems.at[4])
    copy.start()
    copy.wait()
    going = [pltpu.make_async_copy(tiles_ref.at[x], tiles_hbm.at[x], sems.at[x]) for x in range(4)]
    lane = iota((8, LANES), 1)
    for x in range(4):
        parts = [vis_ref[r * 8 : (r + 1) * 8, 0, x * LANES : (x + 1) * LANES] for r in range(4)]
        for b in range(4):
            tile = jnp.zeros((8, LANES), F32)
            for half in range(2):
                for r in range(2):
                    for a in range(REPS):
                        to = half * 64 + r * ROWS + a * OWN
                        moved = pltpu.roll(parts[2 * r + half], (to - (64 * a + 16 * b)) % LANES, 1)
                        tile = jnp.where((lane >> 4) == (to >> 4), moved, tile)
            for a in range(REPS):
                tiles_ref[x ^ (LEAD >> 3), (4 * a + b) ^ (LEAD & 7)] = tile
        going[x ^ (LEAD >> 3)].start()
    for copy in going:
        copy.wait()


def products(model_ref, gains_ref, start, k, lanes=slice(None)):
    half = model_ref.shape[1] // 2
    model_real = model_ref[k, pl.ds(start, OWN), lanes]
    model_imag = model_ref[k, pl.ds(start + half, OWN), lanes]
    col_real = gains_ref[k : k + 1, lanes]
    col_imag = gains_ref[DIRS + k : DIRS + k + 1, lanes]
    return model_real * col_real + model_imag * col_imag, model_imag * col_real - model_real * col_imag


def predict(model_ref, gains_ref, own, start):
    pred_real = jnp.zeros((OWN, STATIONS), F32)
    pred_imag = jnp.zeros((OWN, STATIONS), F32)
    lane = iota((OWN, LANES), 1)
    denom = jnp.zeros((OWN, LANES), F32)
    for k in range(DIRS):
        along_real, along_imag = products(model_ref, gains_ref, start, k)
        row_real = own[:, k : k + 1]
        row_imag = own[:, DIRS + k : DIRS + k + 1]
        pred_real = pred_real + (row_real * along_real - row_imag * along_imag)
        pred_imag = pred_imag + (row_real * along_imag + row_imag * along_real)
        den = jnp.sum(along_real * along_real + along_imag * along_imag, axis=1, keepdims=True)
        denom = jnp.where((lane == k) | (lane == DIRS + k), den, denom)
    return pred_real, pred_imag, denom


def lane_sums(part_ref):
    shape = part_ref.shape
    high, low = split2(part_ref[...].reshape(-1, LANES))
    ones = jnp.ones((LANES, LANES), BF16)
    return (dot(low, ones) + dot(high, ones)).reshape(shape)


def by_lane(real, imag, rows):
    lane = iota((rows, LANES), 1)
    out = jnp.zeros((rows, LANES), F32)
    for k in range(DIRS):
        out = jnp.where(lane == k, real(k), jnp.where(lane == DIRS + k, imag(k), out))
    return out


def pieces_of(t):
    return slice(t * LANES, (t + 1) * LANES)


def row_sums(model_ref, vis_ref, turned, own, start, along_ref, part_ref):
    n = own.shape[0]
    real_rows, imag_rows = pl.ds(start, n), pl.ds(start + ROWS, n)
    pred_real = [jnp.zeros((n, LANES), F32)] * 4
    pred_imag = [jnp.zeros((n, LANES), F32)] * 4
    for k in range(DIRS):
        row_real = jnp.broadcast_to(own[:, k : k + 1], (n, LANES))
        row_imag = jnp.broadcast_to(own[:, DIRS + k : DIRS + k + 1], (n, LANES))
        squares = None
        for t in range(4):
            col_real = turned[32 * t + k : 32 * t + k + 1, :]
            col_imag = turned[32 * t + DIRS + k : 32 * t + DIRS + k + 1, :]
            model_real = model_ref[k, real_rows, pieces_of(t)]
            model_imag = model_ref[k, imag_rows, pieces_of(t)]
            along_real = model_real * col_real + model_imag * col_imag
            along_imag = model_imag * col_real - model_real * col_imag
            along_ref[k, 0:n, pieces_of(t)] = along_real
            along_ref[k, n : 2 * n, pieces_of(t)] = along_imag
            pred_real[t] = pred_real[t] + (row_real * along_real - row_imag * along_imag)
            pred_imag[t] = pred_imag[t] + (row_real * along_imag + row_imag * along_real)
            square = along_real * along_real + along_imag * along_imag
            squares = square if squares is None else squares + square
        part_ref[2, k] = squares
    resid_real = [vis_ref[real_rows, pieces_of(t)] - pred_real[t] for t in range(4)]
    resid_imag = [vis_ref[imag_rows, pieces_of(t)] - pred_imag[t] for t in range(4)]
    correlate(resid_real, resid_imag, lambda k, t: (along_ref[k, 0:n, pieces_of(t)], along_ref[k, n : 2 * n, pieces_of(t)]), part_ref)
    sums = lane_sums(part_ref)
    return by_lane(lambda k: sums[0, k], lambda k: sums[1, k], n), by_lane(lambda k: sums[2, k], lambda k: sums[2, k], n)


def correlate(resid_real, resid_imag, along, part_ref):
    for k in range(DIRS):
        real = imag = None
        for t in range(4):
            along_real, along_imag = along(k, t)
            u = resid_real[t] * along_real + resid_imag[t] * along_imag
            v = resid_imag[t] * along_real - resid_real[t] * along_imag
            real = u if real is None else real + u
            imag = v if imag is None else imag + v
        part_ref[0, k] = real
        part_ref[1, k] = imag


def updated(numer, denom, own, anchor, penalty):
    fresh = (numer + own * denom + penalty * anchor) / (denom + penalty)
    return jnp.where(iota(own.shape, 1) < 2 * DIRS, 0.5 * (own + fresh), 0.0)


def model_kernel(
    offs_hbm, place_hbm, lmn_hbm, flux_hbm, map_hbm, order_hbm, penalty_hbm,
    model_ref, own_ref, table_ref, gains_ref, pred_ref, den_ref, weight_ref,
    offs_ref, xyz_ref, lmn_ref, flux_ref, map_ref, order_ref, penalty_ref, sky_ref, part_ref, sems,
):
    pairs = [
        (map_hbm, map_ref), (lmn_hbm, lmn_ref), (flux_hbm, flux_ref),
        (offs_hbm, offs_ref), (place_hbm, xyz_ref), (penalty_hbm, penalty_ref), (order_hbm, order_ref),
    ]
    copies = [pltpu.make_async_copy(a, b, sems.at[n]) for n, (a, b) in enumerate(pairs)]
    for copy in copies:
        copy.start()
    device = lax.axis_index("stcol")
    scale = 1.0 + 0.5 * lax.axis_index("freq").astype(F32) / CHANNELS
    place = station_at(iota((STATIONS, STATIONS), 0))
    placing = as_table(place == iota((STATIONS, STATIONS), 1))
    column = iota((STATIONS, STATIONS), 0)
    column = ((((column >> 3) & 31) ^ LEAD) << 4) + ((column >> 8) << 3) + (column & 7)
    ordering = as_table(column == iota((STATIONS, STATIONS), 1))
    mine = as_table(iota((ROWS, STATIONS), 1) == row_station((ROWS, STATIONS), 0, device))
    ahead = as_table(iota((LANES, LANES), 0) <= iota((LANES, LANES), 1))
    for copy in copies:
        copy.wait()
    lane = iota((1, LANES), 1)
    weight = jnp.ones((1, LANES), F32)
    for k in range(DIRS):
        weight = jnp.where((lane == k) | (lane == DIRS + k), penalty_ref[0, k], weight)
    weight_ref[...] = weight
    offs = offs_ref[...]
    rows = [1.0 + offs[0:DIRS, :], offs[DIRS : 2 * DIRS, :]] + [xyz_ref[c] for c in range(3)]
    pieces = split3(jnp.concatenate(rows + [jnp.zeros((5, STATIONS), F32)], axis=0))
    moved = chosen(pieces, placing)
    gains_ref[...] = moved[0 : 2 * DIRS, :]
    order = order_ref[...]
    digits = jnp.concatenate([order >> 3, order & 7, jnp.zeros((6, STATIONS), jnp.int32)], axis=0).astype(F32)
    digits = dot_nt(digits.astype(BF16), ordering)
    order = (8.0 * digits[0:1, :] + digits[1:2, :]).astype(jnp.int32)
    table_ref[...] = as_table(place == order)
    own = sum(dot_nt(mine, piece) for piece in pieces[::-1])
    own = jnp.concatenate([own, jnp.zeros((ROWS, LANES - own.shape[1]), F32)], axis=1)
    own_xyz = [scale * own[:, 2 * DIRS + c : 2 * DIRS + c + 1] for c in range(3)]
    own_ref[...] = jnp.where(iota(own.shape, 1) < 2 * DIRS, own, 0.0)
    count = DIRS * SRC
    member = map_ref[...] == iota((DIRS, count), 0)
    member_f = jnp.where(member, 1.0, 0.0)
    blocks = count // LANES
    stacked = jnp.concatenate([member_f[:, b * LANES : (b + 1) * LANES] for b in range(blocks)], axis=0)
    running = dot(stacked.astype(BF16), ahead)
    carried = jnp.zeros((DIRS, 1), F32)
    ranks = []
    for b in range(blocks):
        here = running[b * DIRS : (b + 1) * DIRS, :] + carried
        ranks.append(jnp.sum(here * member_f[:, b * LANES : (b + 1) * LANES], axis=0, keepdims=True))
        carried = here[:, LANES - 1 : LANES]
    rank = jnp.concatenate(ranks, axis=1) - 1.0
    slots = as_table(iota((SRC, count), 0) == rank.astype(jnp.int32))
    values = [lmn_ref[0:1, :], lmn_ref[1:2, :], lmn_ref[2:3, :], flux_ref[...]]
    pieces = [[], [], []]
    for value in values:
        for s, piece in enumerate(split3(value)):
            pieces[s].append(piece.astype(F32) * member_f)
    pieces = [jnp.concatenate(p, axis=0).astype(BF16) for p in pieces]
    along = chosen(pieces, slots)
    down = dot_nt(slots, pieces[2]) + dot_nt(slots, pieces[1]) + dot_nt(slots, pieces[0])
    sky_ref[...] = jnp.concatenate([along, along], axis=1)
    part_ref[...] = down
    xyz = [scale * moved[2 * DIRS + c : 2 * DIRS + c + 1, :] for c in range(3)]
    kept = station_at(iota((ROWS, STATIONS), 1)) != row_station((ROWS, STATIONS), 0, device)
    half = iota((1, LANES), 1) < SRC
    shift_real = jnp.where(half, 0.0, 0.25)
    shift_imag = jnp.where(half, 0.25, 0.5)
    for k in range(DIRS):
        column = [part_ref[:, c * DIRS + k : c * DIRS + k + 1] for c in range(3)]
        turns = wrapped(xyz[0] * column[0] + xyz[1] * column[1] + xyz[2] * column[2])
        wave = jnp.concatenate([cos_turns(turns), sin_turns(turns)], axis=0)
        wave_high, wave_low = split2(wave)
        row = [sky_ref[c * DIRS + k : c * DIRS + k + 1, :] for c in range(4)]
        turns = wrapped(own_xyz[0] * row[0] + own_xyz[1] * row[1] + own_xyz[2] * row[2])
        near = jnp.concatenate([cos_turns(wrapped(turns - shift_real)), cos_turns(wrapped(turns - shift_imag))], axis=0)
        near_high, near_low = split2(near * row[3])
        model = dot(near_high, wave_low) + dot(near_low, wave_high) + dot(near_high, wave_high)
        model_ref[k, 0:ROWS, :] = jnp.where(kept, model[0:ROWS, :], 0.0)
        model_ref[k, ROWS : 2 * ROWS, :] = jnp.where(kept, model[ROWS:, :], 0.0)
    for a in range(REPS):
        rows = slice(a * OWN, (a + 1) * OWN)
        pred_real, pred_imag, denom = predict(model_ref, gains_ref, own_ref[rows, :], a * OWN)
        pred_ref[rows, :] = pred_real
        pred_ref[ROWS + a * OWN : ROWS + (a + 1) * OWN, :] = pred_imag
        den_ref[rows, :] = denom


def channel_fit(near_ref, far_ref):
    channel = lax.axis_index("freq")
    total = None
    for d in range(CHANNELS // 2):
        other = channel ^ (2 * d)
        for tiles_ref, source in ((near_ref, other), (far_ref, other ^ 1)):
            part = channel_weight(channel, source) * tiles_ref[d]
            total = part if total is None else total + part
    return unpacked(total)


def sums(model_ref, vis_ref, tiles_ref, own_ref, numer_ref, den_ref, along_ref, part_ref):
    turned = jnp.transpose(tiles_ref[...])
    numer_ref[...], den_ref[...] = row_sums(model_ref, vis_ref, turned, own_ref[...], 0, along_ref, part_ref)


def first_kernel(
    tiles_ref, table_ref, model_ref, gains_ref, pred_ref, den_ref, own_ref, penalty_ref, vis_ref, state_ref, send_ref, part_ref
):
    turned = jnp.transpose(tiles_ref[...])
    pieces = split3(jnp.concatenate([turned[0 : 2 * ROWS, :], turned[2 * ROWS :, :]], axis=1))
    vis_ref[...] = chosen(pieces, table_ref[...])
    for a in range(REPS):
        rows = slice(a * OWN, (a + 1) * OWN)
        lower = slice(ROWS + a * OWN, ROWS + (a + 1) * OWN)
        resid_real = [vis_ref[rows, pieces_of(t)] - pred_ref[rows, pieces_of(t)] for t in range(4)]
        resid_imag = [vis_ref[lower, pieces_of(t)] - pred_ref[lower, pieces_of(t)] for t in range(4)]
        correlate(resid_real, resid_imag, lambda k, t: products(model_ref, gains_ref, a * OWN, k, pieces_of(t)), part_ref)
        total = [[jnp.sum(part_ref[r, k], axis=1, keepdims=True) for k in range(DIRS)] for r in range(2)]
        numer = by_lane(lambda k: total[0][k], lambda k: total[1][k], OWN)
        own = own_ref[rows, :]
        state_ref[rows, :] = updated(numer, den_ref[rows, :], own, own, penalty_ref[...])
    send_ref[...] = packed(state_ref[...])


def second_kernel(
    model_ref, vis_ref, tiles_ref, own_ref, anchor_ref, penalty_ref, state_ref, send_ref, along_ref, part_ref
):
    turned = jnp.transpose(tiles_ref[...])
    own = own_ref[...]
    numer, denom = row_sums(model_ref, vis_ref, turned, own, 0, along_ref, part_ref)
    state = updated(numer, denom, own, anchor_ref[...], penalty_ref[...])
    state_ref[...] = state
    send_ref[...] = packed(state)


def anchor_kernel(numer_ref, den_ref, near_ref, far_ref, own_ref, penalty_ref, state_ref, anchor_ref, dual_ref, send_ref):
    own = own_ref[...]
    cons = channel_fit(near_ref, far_ref)
    dual = own - cons
    anchor = cons - dual
    state = updated(numer_ref[...], den_ref[...], own, anchor, penalty_ref[...])
    state_ref[...] = state
    send_ref[...] = packed(state)
    anchor_ref[...] = anchor
    dual_ref[...] = dual


def by_direction(state):
    filled = jnp.concatenate([state, jnp.zeros((LANES - OWN, LANES), F32)], axis=0)
    return jnp.transpose(filled)[0 : 2 * DIRS, 0:OWN]


def fourth_kernel(
    model_ref, vis_ref, tiles_ref, own_ref, anchor_ref, dual_ref, penalty_ref, state_ref, send_ref, along_ref, part_ref
):
    start = pl.multiple_of(rep_of(lax.axis_index("stcol")) * OWN, OWN)
    rows = pl.ds(start, OWN)
    own = own_ref[rows, :]
    turned = jnp.transpose(tiles_ref[...])
    numer, denom = row_sums(model_ref, vis_ref, turned, own, start, along_ref, part_ref)
    state = updated(numer, denom, own, anchor_ref[rows, :], penalty_ref[...])
    state_ref[...] = state
    send_ref[...] = packed(state + dual_ref[rows, :])


def last_kernel(tiles_ref, state_ref, out_ref, cons_ref):
    out_ref[...] = by_direction(state_ref[...])
    channel = lax.axis_index("freq")
    total = basis_product(channel, HEAD) * tiles_ref[0]
    for f in range(1, CHANNELS):
        total = total + basis_product(channel, f ^ HEAD) * tiles_ref[f]
    cons_ref[...] = by_direction(unpacked(total))


def called(kernel, outs, scratch=(), name=None, in_specs=None, out_specs=None):
    return pl.pallas_call(
        kernel,
        out_shape=[jax.ShapeDtypeStruct(*o) for o in outs],
        scratch_shapes=[pltpu.VMEM(*o) if isinstance(o, tuple) else o for o in scratch],
        compiler_params=pltpu.CompilerParams(vmem_limit_bytes=32 * 1024 * 1024),
        name=name,
        **({} if in_specs is None else {"in_specs": in_specs}),
        **({} if out_specs is None else {"out_specs": out_specs}),
    )


def held(x):
    return pltpu.with_memory_space_constraint(x, pltpu.HBM)


def to_all(tile, axis, count, groups=None):
    tiles = jnp.broadcast_to(tile, (count, *tile.shape))
    return lax.all_to_all(tiles, axis, 0, 0, tiled=True, axis_index_groups=groups)


def around(tile):
    swaps = {d: lax.ppermute(tile, "freq", [(i, i ^ (2 * d)) for i in range(CHANNELS)]) for d in (1, 3, 2)}
    return [tile, swaps[1], swaps[2], swaps[3]]


def both_cores(tiles):
    near = jnp.stack(tiles)
    return near, lax.ppermute(near, "freq", [(i, i ^ 1) for i in range(CHANNELS)])


def to_members(tile):
    members = [e ^ FRONT for e in range(MEMBERS)]
    groups = [[(e >> 2) * 8 + 4 * m + (e & 3) for e in members] for m in range(REPS)]
    return to_all(tile, "stcol", MEMBERS, groups).reshape(LANES, LANES)


def on_device(visibilities, positions, source_lmn, source_flux, cluster_map, station_order, penalty, offsets):
    hbm = pl.BlockSpec(memory_space=pltpu.HBM)
    model_out = ((DIRS, 2 * ROWS, STATIONS), F32)
    along = ((DIRS, 2 * OWN, STATIONS), F32)
    part = ((3, DIRS, OWN, LANES), F32)
    parts = ((3, DIRS, ROWS, LANES), F32)
    vis_out = ((2 * ROWS, STATIONS), F32)
    state_out = ((ROWS, LANES), F32)
    send_out = ((ROWS // 4, LANES), F32)
    flat_out = ((2 * DIRS, OWN), F32)
    gains_out = ((2 * DIRS, STATIONS), F32)
    (tiles,) = called(
        turn_kernel,
        [((4, 8, 8, LANES), F32)],
        [((2 * OWN, 1, STATIONS), F32), ((4, 8, 8, LANES), F32), pltpu.SemaphoreType.DMA((5,))],
        "turn",
        [hbm],
        [hbm],
    )(held(visibilities.reshape(2 * OWN, 1, STATIONS)))
    slots = [s ^ LEAD for s in range(STATIONS // OWN)]
    tiles = lax.all_to_all(tiles.reshape(STATIONS // OWN, 8, LANES), "stcol", 0, 0, tiled=True, axis_index_groups=[slots]).reshape(STATIONS // 2, LANES)
    count = DIRS * SRC
    model, own, table, gains, pred, den, pen = called(
        model_kernel,
        [model_out, state_out, ((STATIONS, STATIONS), BF16), gains_out, vis_out, state_out, ((1, LANES), F32)],
        [
            gains_out, ((3, 1, STATIONS), F32), ((3, count), F32), ((1, count), F32), ((1, count), jnp.int32),
            ((1, STATIONS), jnp.int32), pltpu.SMEM((1, DIRS), F32), ((4 * DIRS, 2 * SRC), F32), ((SRC, 4 * DIRS), F32),
            pltpu.SemaphoreType.DMA((7,)),
        ],
        "models",
        [hbm] * 7,
    )(
        held(offsets.reshape(2 * DIRS, STATIONS)), held(positions), held(source_lmn), held(source_flux.reshape(1, count)),
        held(cluster_map.reshape(1, count)), held(station_order.reshape(1, STATIONS)), held(penalty.reshape(1, DIRS)),
    )
    vis, state, send = called(first_kernel, [vis_out, state_out, send_out], [((2, DIRS, OWN, LANES), F32)], "pass_one")(
        tiles, table, model, gains, pred, den, own, pen
    )
    got = to_members(send)
    state, send = called(second_kernel, [state_out, send_out], [model_out, parts], "pass_two")(
        model, vis, got, state, own, pen
    )
    tiles = around(send)
    got = to_members(send)
    numer, den = called(sums, [state_out, state_out], [model_out, parts], "pass_three")(model, vis, got, state)
    near, far = both_cores(lax.optimization_barrier((*tiles, got))[:-1])
    state, anchor, dual, send = called(anchor_kernel, [state_out, state_out, state_out, send_out], name="update_three")(
        numer, den, near, far, state, pen
    )
    got = to_members(send)
    state, send = called(fourth_kernel, [((OWN, LANES), F32), ((4, LANES), F32)], [along, part], "pass_four")(
        model, vis, got, state, anchor, dual, pen
    )
    out, cons = called(last_kernel, [flat_out, flat_out], name="consensus")(to_all(send, "freq", CHANNELS, [[f ^ HEAD for f in range(CHANNELS)]]), state)
    shape = (2, 1, DIRS, OWN)
    return out.reshape(shape), cons.reshape(shape)


def solution(mesh):
    in_specs = (
        P(None, "freq", "stcol", None, None),
        P(),
        P(),
        P(),
        P(),
        P(),
        P(),
        P(None, "freq", None, None),
    )
    out_specs = (P(None, "freq", None, "stcol"), P(None, "freq", None, "stcol"))
    return jax.shard_map(
        on_device, mesh=mesh, in_specs=in_specs, out_specs=out_specs, check_vma=False
    )
```
